256 devices in a mesh: seg: 32 (over y, x, core), fft: 8 (over z).
Axes of the slice: x: 4, y: 4, z: 8, core: 2. Of those that a mesh axis runs over, the one named last changes fastest.
Arguments:
- voltage: float32 [32, 2, 256, 4096], P('seg', None, None, 'fft'), may hold values from -6 to 6
- chirp_phase: float32 [2, 512, 4096], P(None, 'fft'), may hold values from -3.140625 to 3.140625
Outputs:
- dedispersed: float32 [32, 2, 256, 4096], P('seg', None, None, 'fft')
The draws below stay inside these ranges and needn't reach their ends.
All inputs are finite; a program needn't handle non-finite values.
Results may differ from the reference program's by a relative error of at most 0.0001.
Values sent between devices are 32-bit elements; how exact they have to be, the bound alone decides.
A program may use at most 128 MiB of HBM per device.

```python
import jax
import jax.numpy as jnp
from jax import lax

M = 8388608
A = 1024
B = 4096
L = 2097152
SEGS = 32


def block_scale(key, extent, cuts, least, top_value):
    def one(position, blocks):
        heights = jax.random.uniform(jax.random.fold_in(jax.random.fold_in(key, 6), position), (blocks,), jnp.float32, least / len(cuts), top_value / len(cuts))
        return jnp.repeat(jnp.exp(heights), extent[position] // blocks).reshape((-1,) + (1,) * (len(extent) - position - 1))

    loudness = one(*cuts[0])
    for cut in cuts[1:]:
        loudness = loudness * one(*cut)
    return loudness


def scatter_about(own_key, shape, width, reach, pieces=(), held_as=jnp.bfloat16):
    gain = block_scale(own_key, shape, pieces, -0.22, 0.18) if pieces else 1.0
    result = jax.random.normal(own_key, shape, jnp.float32) * width * gain
    return jnp.minimum(jnp.maximum(result, -reach), reach).astype(held_as)


def setup_inputs(seed: int = 0) -> dict:
    streams_of = jax.random.split(jax.random.key(seed), 3)
    voltage = scatter_about(streams_of[0], (SEGS, 2, A // 4, B), 1.0, 6.0, ((0, 32), (3, 8)), jnp.float32)
    chirp_phase = jnp.clip(jax.random.uniform(streams_of[1], (2, A // 2, B), jnp.float32, -3.140625, 3.140625), -3.140625, 3.140625)
    return {"voltage": voltage, "chirp_phase": chirp_phase}


def unfold_chirp(chirp_phase):
    natural = jnp.concatenate([chirp_phase[0], chirp_phase[1, :1], jnp.flip(chirp_phase[1, 1:], axis=0)], axis=0)
    return jnp.transpose(natural).reshape(-1)


def reference(voltage, chirp_phase):
    phase_flat = unfold_chirp(chirp_phase)
    chirp_real = jnp.cos(phase_flat)
    chirp_imag = jnp.sin(phase_flat)
    keep_bins = jnp.arange(M // 2) > 0

    def advance(pending, samples):
        series = jnp.transpose(samples, (1, 2, 0)).reshape(L)
        padded = jnp.concatenate([series, jnp.zeros((M - L,), series.dtype)])
        spectrum = jnp.fft.rfft(padded)[: M // 2]
        spec_real = jnp.real(spectrum)
        spec_imag = jnp.imag(spectrum)
        filt_real = jnp.where(keep_bins, spec_real * chirp_real - spec_imag * chirp_imag, 0.0)
        filt_imag = jnp.where(keep_bins, spec_real * chirp_imag + spec_imag * chirp_real, 0.0)
        closing = jnp.zeros((1,), filt_real.dtype)
        filtered = lax.complex(jnp.concatenate([filt_real, closing]), jnp.concatenate([filt_imag, closing]))
        blocks = jnp.fft.irfft(filtered, n=M).reshape(4, L)
        emitted = blocks[0] + pending[0]
        carried = jnp.stack([pending[1] + blocks[1], pending[2] + blocks[2], blocks[3]])
        return carried, emitted

    start = jnp.zeros((3, L), jnp.float32)
    leftover, emitted = lax.scan(advance, start, voltage)
    shaped = emitted.reshape(SEGS, A // 4, B, 2)
    return jnp.transpose(shaped, (0, 3, 1, 2)).astype(jnp.float32)
```

```python
import math

import jax
import jax.numpy as jnp
from jax import lax
from jax.sharding import PartitionSpec as P

B1 = 64


HIGHEST = lax.Precision.HIGHEST


def passed_along(shard, axis, by):
    length = lax.axis_size(axis)
    pairs = [(i, i + by) for i in range(length) if 0 <= i + by < length]
    return lax.ppermute(shard, axis, pairs)


def rotation(products, period):
    reduced = jnp.mod(products, period).astype(jnp.float32)
    angles = reduced * jnp.float32(-2.0 * math.pi / period)
    return jnp.stack([jnp.cos(angles), jnp.sin(angles)])


def conjugate(pair):
    return jnp.stack([pair[0], -pair[1]])


def real_table(pair):
    return jnp.stack([jnp.stack([pair[0], pair[1]]), jnp.stack([-pair[1], pair[0]])])


def complex_mul(left_pair, right_pair):
    first = left_pair[0] * right_pair[0] - left_pair[1] * right_pair[1]
    second = left_pair[0] * right_pair[1] + left_pair[1] * right_pair[0]
    return jnp.stack([first, second])


def fold_order(row_count, groups):
    half_count = row_count // (2 * groups)
    places = jnp.arange(row_count, dtype=jnp.int32)
    within = places % (2 * half_count)
    base_row = places // (2 * half_count) * half_count + within % half_count
    mirror_row = jnp.where(base_row > 0, row_count - base_row, row_count // 2)
    return jnp.where(within >= half_count, mirror_row, base_row)


def both_halves(outer, inner, period, reverse_outer, reverse_inner):
    last_outer = outer.shape[0] - 1
    last_inner = inner.shape[0] - 1
    natural = outer[:, None] * inner[None, :]
    outer_turned = (last_outer - outer) if reverse_outer else outer
    inner_turned = (last_inner - inner) if reverse_inner else inner
    turned = outer_turned[:, None] * inner_turned[None, :]
    return jnp.stack([rotation(natural, period), rotation(turned, period)], axis=1)


def reverse_lanes(values):
    width = values.shape[-1]
    tiles = values.reshape(values.shape[:-1] + (width // 128, 128))
    tiles = jnp.flip(tiles, axis=-2)
    lane = jnp.arange(128, dtype=jnp.int32)
    anti = (lane[:, None] + lane[None, :] == 127).astype(jnp.float32)
    flipped = jnp.einsum("...l,lm->...m", tiles, anti, precision=HIGHEST)
    return flipped.reshape(values.shape)


def partners(base, mirror, is_first):
    first_base = jnp.roll(reverse_lanes(base[:, 0]), 1, axis=-1)
    first_mirror = reverse_lanes(mirror[:, 0])
    of_base = mirror.at[:, 0].set(jnp.where(is_first, first_base, mirror[:, 0]))
    of_mirror = base.at[:, 0].set(jnp.where(is_first, first_mirror, base[:, 0]))
    return of_base, of_mirror


def per_device(voltage, chirp_phase):
    groups = lax.axis_size("fft")
    device = lax.axis_index("fft")
    quarter = voltage.shape[2]
    row_count = 4 * quarter
    local_width = voltage.shape[3]
    columns = local_width * groups
    second_len = columns // B1
    total_bins = row_count * columns
    half_count = row_count // (2 * groups)
    local_rows = 2 * half_count
    is_first = device == 0
    row_order = fold_order(row_count, groups)
    local_order = lax.dynamic_slice_in_dim(row_order, device * local_rows, local_rows)
    first_range = jnp.arange(B1, dtype=jnp.int32)
    second_range = jnp.arange(second_len, dtype=jnp.int32)
    column_range = jnp.arange(columns, dtype=jnp.int32)
    sample_rows = jnp.arange(quarter, dtype=jnp.int32)
    entry_table = real_table(rotation(sample_rows[:, None] * row_order[None, :], row_count))
    spread = jnp.einsum("pmb,pqmr->qrb", voltage[0], entry_table, precision=HIGHEST)
    local_columns = device * local_width + jnp.arange(local_width, dtype=jnp.int32)
    spread = complex_mul(spread, rotation(row_order[:, None] * local_columns[None, :], total_bins))
    spread = spread.reshape(2, row_count, B1 // groups, second_len)
    gathered = lax.all_to_all(spread, "fft", split_axis=1, concat_axis=2, tiled=True)
    gathered = gathered.reshape(2, 2, half_count, B1, second_len)
    section_one = both_halves(first_range, first_range, B1, False, True)
    block_turn = both_halves(first_range, second_range, columns, True, False)
    section_two = both_halves(second_range, second_range, second_len, False, True)
    gathered = jnp.einsum("phrun,pqhuk->qhrkn", gathered, real_table(section_one), precision=HIGHEST)
    gathered = complex_mul(gathered, block_turn[:, :, None])
    spectrum = jnp.einsum("phrkn,pqhnj->qhrjk", gathered, real_table(section_two), precision=HIGHEST)
    spectrum = spectrum.reshape(2, 2, half_count, columns)
    base_rows = local_order[:half_count]
    mirror_rows = local_order[half_count:]
    base_bins = base_rows[:, None] + row_count * column_range[None, :]
    mirror_bins = mirror_rows[:, None] + row_count * (columns - 1 - column_range[None, :])
    bins = jnp.stack([base_bins, mirror_bins])
    bin_turn = rotation(bins, 2 * total_bins)
    of_base, of_mirror = partners(spectrum[:, 0], spectrum[:, 1], is_first)
    partner = conjugate(jnp.stack([of_base, of_mirror], axis=1))
    even_spec = 0.5 * (spectrum + partner)
    odd_spec = jnp.stack([0.5 * (spectrum[1] - partner[1]), -0.5 * (spectrum[0] - partner[0])])
    transformed = even_spec + complex_mul(odd_spec, bin_turn)
    phase_rows = jnp.stack([chirp_phase[0], reverse_lanes(chirp_phase[1])])
    filtered = complex_mul(transformed, jnp.stack([jnp.cos(phase_rows), jnp.sin(phase_rows)]))
    live_bins = bins > 0
    filtered = jnp.where(live_bins[None], filtered, 0.0)
    of_base, of_mirror = partners(filtered[:, 0], filtered[:, 1], is_first)
    partner = conjugate(jnp.stack([of_base, of_mirror], axis=1))
    even_back = 0.5 * (filtered + partner)
    odd_back = complex_mul(0.5 * (filtered - partner), conjugate(bin_turn))
    packed = jnp.stack([even_back[0] - odd_back[1], even_back[1] + odd_back[0]])
    packed = packed.reshape(2, 2, half_count, second_len, B1)
    back_two = both_halves(second_range, second_range, second_len, True, False)
    back_turn = both_halves(first_range, second_range, columns, True, False)
    back_one = both_halves(first_range, first_range, B1, True, False)
    packed = jnp.einsum(
        "phrjk,pqhjv->qhrkv", packed, real_table(conjugate(back_two)), precision=HIGHEST
    )
    packed = complex_mul(packed, conjugate(back_turn)[:, :, None])
    packed = jnp.einsum(
        "phrkv,pqhku->qhruv", packed, real_table(conjugate(back_one)), precision=HIGHEST
    )
    packed = packed.reshape(2, local_rows, columns)
    packed = complex_mul(
        packed, conjugate(rotation(local_order[:, None] * column_range[None, :], total_bins))
    )
    packed = packed.reshape(2, local_rows, groups, local_width)
    arrived = lax.all_to_all(packed, "fft", split_axis=2, concat_axis=1, tiled=True)
    arrived = arrived.reshape(2, row_count, local_width)
    exit_turn = rotation(
        row_order[:, None] * jnp.arange(row_count, dtype=jnp.int32)[None, :], row_count
    )
    exit_table = real_table(jnp.stack([exit_turn[0] / total_bins, -exit_turn[1] / total_bins]))

    def sample_block(block_id):
        lower = block_id * quarter
        table = exit_table[:, :, :, lower : lower + quarter]
        return jnp.einsum("prn,pqrm->qmn", arrived, table, precision=HIGHEST)

    tails = [passed_along(sample_block(block_id), "seg", block_id) for block_id in (3, 2, 1)]
    running = sample_block(0)
    for tail in tails[::-1]:
        running = running + tail
    return running[None]


def solution(mesh):
    in_specs = (P("seg", None, None, "fft"), P(None, "fft", None))
    out_specs = P("seg", None, None, "fft")
    return jax.shard_map(
        per_device, mesh=mesh, in_specs=in_specs, out_specs=out_specs, check_vma=False
    )
```

```python
import math

import jax
import jax.numpy as jnp
from jax import lax
from jax.experimental import pallas as pl
from jax.sharding import PartitionSpec as P

B1 = 64
TILE_ROWS = 8


HIGHEST = lax.Precision.HIGHEST


def passed_along(shard, axis, by):
    length = lax.axis_size(axis)
    pairs = [(i, i + by) for i in range(length) if 0 <= i + by < length]
    return lax.ppermute(shard, axis, pairs)


def rotation(products, period):
    reduced = jnp.mod(products, period).astype(jnp.float32)
    angles = reduced * jnp.float32(-2.0 * math.pi / period)
    return jnp.stack([jnp.cos(angles), jnp.sin(angles)])


def conjugate(pair):
    return jnp.stack([pair[0], -pair[1]])


def real_table(pair):
    return jnp.stack([jnp.stack([pair[0], pair[1]]), jnp.stack([-pair[1], pair[0]])])


def complex_mul(left_pair, right_pair):
    first = left_pair[0] * right_pair[0] - left_pair[1] * right_pair[1]
    second = left_pair[0] * right_pair[1] + left_pair[1] * right_pair[0]
    return jnp.stack([first, second])


def fold_order(row_count, groups):
    half_count = row_count // (2 * groups)
    places = jnp.arange(row_count, dtype=jnp.int32)
    within = places % (2 * half_count)
    base_row = places // (2 * half_count) * half_count + within % half_count
    mirror_row = jnp.where(base_row > 0, row_count - base_row, row_count // 2)
    return jnp.where(within >= half_count, mirror_row, base_row)


def both_halves(outer, inner, period, reverse_outer, reverse_inner):
    last_outer = outer.shape[0] - 1
    last_inner = inner.shape[0] - 1
    natural = outer[:, None] * inner[None, :]
    outer_turned = (last_outer - outer) if reverse_outer else outer
    inner_turned = (last_inner - inner) if reverse_inner else inner
    turned = outer_turned[:, None] * inner_turned[None, :]
    return jnp.stack([rotation(natural, period), rotation(turned, period)], axis=1)


def reverse_lanes(values):
    width = values.shape[-1]
    tiles = values.reshape(values.shape[:-1] + (width // 128, 128))
    tiles = jnp.flip(tiles, axis=-2)
    lane = jnp.arange(128, dtype=jnp.int32)
    anti = (lane[:, None] + lane[None, :] == 127).astype(jnp.float32)
    flipped = jnp.einsum("...l,lm->...m", tiles, anti, precision=HIGHEST)
    return flipped.reshape(values.shape)


def partners(base, mirror, is_first):
    first_base = jnp.roll(reverse_lanes(base[:, 0]), 1, axis=-1)
    first_mirror = reverse_lanes(mirror[:, 0])
    of_base = mirror.at[:, 0].set(jnp.where(is_first, first_base, mirror[:, 0]))
    of_mirror = base.at[:, 0].set(jnp.where(is_first, first_mirror, base[:, 0]))
    return of_base, of_mirror


def post_process(spec, partner, turn):
    even = 0.5 * (spec + partner)
    odd = jnp.stack([0.5 * (spec[1] - partner[1]), -0.5 * (spec[0] - partner[0])])
    return even + complex_mul(odd, turn)


def pre_process(filtered, partner, turn):
    even_back = 0.5 * (filtered + partner)
    odd_back = complex_mul(0.5 * (filtered - partner), conjugate(turn))
    return jnp.stack([even_back[0] - odd_back[1], even_back[1] + odd_back[0]])


def middle_kernel(spec_ref, phase_ref, row_ref, column_ref, out_ref):
    turn_re = row_ref[0] * column_ref[0] - row_ref[1] * column_ref[1]
    turn_im = row_ref[0] * column_ref[1] + row_ref[1] * column_ref[0]
    filtered = []
    for half in (0, 1):
        other = 1 - half
        spec = jnp.stack([spec_ref[0, half], spec_ref[1, half]])
        partner = jnp.stack([spec_ref[0, other], -spec_ref[1, other]])
        turn = jnp.stack([turn_re[half], turn_im[half]])
        transformed = post_process(spec, partner, turn)
        phase = phase_ref[half]
        filtered.append(complex_mul(transformed, jnp.stack([jnp.cos(phase), jnp.sin(phase)])))
    for half in (0, 1):
        other = filtered[1 - half]
        turn = jnp.stack([turn_re[half], turn_im[half]])
        packed = pre_process(filtered[half], conjugate(other), turn)
        out_ref[0, half] = packed[0]
        out_ref[1, half] = packed[1]


def middle(spectrum, phase_rows, row_turn, column_turn):
    rows = spectrum.shape[2]
    columns = spectrum.shape[3]
    spec_block = pl.BlockSpec((2, 2, TILE_ROWS, columns), lambda i: (0, 0, i, 0))
    return pl.pallas_call(
        middle_kernel,
        out_shape=jax.ShapeDtypeStruct(spectrum.shape, jnp.float32),
        grid=(rows // TILE_ROWS,),
        in_specs=[
            spec_block,
            pl.BlockSpec((2, TILE_ROWS, columns), lambda i: (0, i, 0)),
            pl.BlockSpec((2, 2, TILE_ROWS, 1), lambda i: (0, 0, i, 0)),
            pl.BlockSpec((2, 2, 1, columns), lambda i: (0, 0, 0, 0)),
        ],
        out_specs=spec_block,
    )(spectrum, phase_rows, row_turn, column_turn)


def per_device(voltage, chirp_phase):
    groups = lax.axis_size("fft")
    device = lax.axis_index("fft")
    quarter = voltage.shape[2]
    row_count = 4 * quarter
    local_width = voltage.shape[3]
    columns = local_width * groups
    second_len = columns // B1
    total_bins = row_count * columns
    half_count = row_count // (2 * groups)
    local_rows = 2 * half_count
    is_first = device == 0
    row_order = fold_order(row_count, groups)
    local_order = lax.dynamic_slice_in_dim(row_order, device * local_rows, local_rows)
    first_range = jnp.arange(B1, dtype=jnp.int32)
    second_range = jnp.arange(second_len, dtype=jnp.int32)
    column_range = jnp.arange(columns, dtype=jnp.int32)
    sample_rows = jnp.arange(quarter, dtype=jnp.int32)
    entry_table = real_table(rotation(sample_rows[:, None] * row_order[None, :], row_count))
    spread = jnp.einsum("pmb,pqmr->qrb", voltage[0], entry_table, precision=HIGHEST)
    spread = spread.reshape(2, row_count, B1 // groups, second_len)
    device_turn = rotation(row_order * (device * local_width), total_bins)
    block_range = jnp.arange(B1 // groups, dtype=jnp.int32)
    within_turn = rotation(row_order[:, None] * (second_len * block_range)[None, :], total_bins)
    inner_turn = rotation(row_order[:, None] * second_range[None, :], total_bins)
    outer_turn = complex_mul(device_turn[:, :, None], within_turn)
    spread = complex_mul(complex_mul(spread, outer_turn[..., None]), inner_turn[:, :, None, :])
    gathered = lax.all_to_all(spread, "fft", split_axis=1, concat_axis=2, tiled=True)
    gathered = gathered.reshape(2, 2, half_count, B1, second_len)
    section_one = both_halves(first_range, first_range, B1, False, True)
    block_turn = both_halves(first_range, second_range, columns, True, False)
    section_two = both_halves(second_range, second_range, second_len, False, True)
    gathered = jnp.einsum("phrun,pqhuk->qhrkn", gathered, real_table(section_one), precision=HIGHEST)
    gathered = complex_mul(gathered, block_turn[:, :, None])
    spectrum = jnp.einsum("phrkn,pqhnj->qhrjk", gathered, real_table(section_two), precision=HIGHEST)
    spectrum = spectrum.reshape(2, 2, half_count, columns)
    half_rows = jnp.stack([local_order[:half_count], local_order[half_count:]])
    row_turn = rotation(half_rows, 2 * total_bins)[..., None]
    stored_columns = jnp.stack([column_range, columns - 1 - column_range])
    column_turn = rotation(stored_columns, 2 * columns)[:, :, None, :]
    phase_rows = jnp.stack([chirp_phase[0], reverse_lanes(chirp_phase[1])])
    packed = middle(spectrum, phase_rows, row_turn, column_turn)
    first_spec = spectrum[:, :, 0]
    first_turn = complex_mul(row_turn[:, :, 0], column_turn[:, :, 0])
    live = jnp.stack([column_range > 0, column_range >= 0])
    first_partner = jnp.stack(
        [jnp.roll(reverse_lanes(first_spec[:, 0]), 1, axis=-1), reverse_lanes(first_spec[:, 1])], axis=1
    )
    first_filtered = complex_mul(
        post_process(first_spec, conjugate(first_partner), first_turn),
        jnp.stack([jnp.cos(phase_rows[:, 0]), jnp.sin(phase_rows[:, 0])]),
    )
    first_filtered = jnp.where(live[None], first_filtered, 0.0)
    first_partner = jnp.stack(
        [jnp.roll(reverse_lanes(first_filtered[:, 0]), 1, axis=-1), reverse_lanes(first_filtered[:, 1])],
        axis=1,
    )
    first_packed = pre_process(first_filtered, conjugate(first_partner), first_turn)
    packed = packed.at[:, :, 0].set(jnp.where(is_first, first_packed, packed[:, :, 0]))
    packed = packed.reshape(2, 2, half_count, second_len, B1)
    back_two = both_halves(second_range, second_range, second_len, True, False)
    back_turn = both_halves(first_range, second_range, columns, True, False)
    back_one = both_halves(first_range, first_range, B1, True, False)
    packed = jnp.einsum(
        "phrjk,pqhjv->qhrkv", packed, real_table(conjugate(back_two)), precision=HIGHEST
    )
    packed = complex_mul(packed, conjugate(back_turn)[:, :, None])
    packed = jnp.einsum(
        "phrkv,pqhku->qhruv", packed, real_table(conjugate(back_one)), precision=HIGHEST
    )
    packed = packed.reshape(2, local_rows, B1, second_len)
    upper_turn = rotation(local_order[:, None] * (second_len * first_range)[None, :], total_bins)
    lower_turn = rotation(local_order[:, None] * second_range[None, :], total_bins)
    packed = complex_mul(
        complex_mul(packed, conjugate(upper_turn)[..., None]), conjugate(lower_turn)[:, :, None, :]
    )
    packed = packed.reshape(2, local_rows, groups, local_width)
    arrived = lax.all_to_all(packed, "fft", split_axis=2, concat_axis=1, tiled=True)
    arrived = arrived.reshape(2, row_count, local_width)
    exit_turn = rotation(
        row_order[:, None] * jnp.arange(row_count, dtype=jnp.int32)[None, :], row_count
    )
    exit_table = real_table(jnp.stack([exit_turn[0] / total_bins, -exit_turn[1] / total_bins]))

    def sample_block(block_id):
        lower = block_id * quarter
        table = exit_table[:, :, :, lower : lower + quarter]
        return jnp.einsum("prn,pqrm->qmn", arrived, table, precision=HIGHEST)

    running = sample_block(3)
    for block_id in (2, 1, 0):
        running = sample_block(block_id) + passed_along(running, "seg", 1)
    return running[None]


def solution(mesh):
    in_specs = (P("seg", None, None, "fft"), P(None, "fft", None))
    out_specs = P("seg", None, None, "fft")
    return jax.shard_map(
        per_device, mesh=mesh, in_specs=in_specs, out_specs=out_specs, check_vma=False
    )
```

```python
import math

import jax
import jax.numpy as jnp
from jax import lax
from jax.experimental import pallas as pl
from jax.sharding import PartitionSpec as P

B1 = 64
TILE_ROWS = 8
CHUNKS = 2


HIGHEST = lax.Precision.HIGHEST


def passed_along(shard, axis, by):
    length = lax.axis_size(axis)
    pairs = [(i, i + by) for i in range(length) if 0 <= i + by < length]
    return lax.ppermute(shard, axis, pairs)


def rotation(products, period):
    reduced = jnp.mod(products, period).astype(jnp.float32)
    angles = reduced * jnp.float32(-2.0 * math.pi / period)
    return jnp.stack([jnp.cos(angles), jnp.sin(angles)])


def conjugate(pair):
    return jnp.stack([pair[0], -pair[1]])


def real_table(pair):
    return jnp.stack([jnp.stack([pair[0], pair[1]]), jnp.stack([-pair[1], pair[0]])])


def complex_mul(left_pair, right_pair):
    first = left_pair[0] * right_pair[0] - left_pair[1] * right_pair[1]
    second = left_pair[0] * right_pair[1] + left_pair[1] * right_pair[0]
    return jnp.stack([first, second])


def fold_order(row_count, groups):
    half_count = row_count // (2 * groups)
    places = jnp.arange(row_count, dtype=jnp.int32)
    within = places % (2 * half_count)
    base_row = places // (2 * half_count) * half_count + within % half_count
    mirror_row = jnp.where(base_row > 0, row_count - base_row, row_count // 2)
    return jnp.where(within >= half_count, mirror_row, base_row)


def both_halves(outer, inner, period, reverse_outer, reverse_inner):
    last_outer = outer.shape[0] - 1
    last_inner = inner.shape[0] - 1
    natural = outer[:, None] * inner[None, :]
    outer_turned = (last_outer - outer) if reverse_outer else outer
    inner_turned = (last_inner - inner) if reverse_inner else inner
    turned = outer_turned[:, None] * inner_turned[None, :]
    return jnp.stack([rotation(natural, period), rotation(turned, period)], axis=1)


def reverse_lanes(values):
    width = values.shape[-1]
    tiles = values.reshape(values.shape[:-1] + (width // 128, 128))
    tiles = jnp.flip(tiles, axis=-2)
    lane = jnp.arange(128, dtype=jnp.int32)
    anti = (lane[:, None] + lane[None, :] == 127).astype(jnp.float32)
    flipped = jnp.einsum("...l,lm->...m", tiles, anti, precision=HIGHEST)
    return flipped.reshape(values.shape)


def partners(base, mirror, is_first):
    first_base = jnp.roll(reverse_lanes(base[:, 0]), 1, axis=-1)
    first_mirror = reverse_lanes(mirror[:, 0])
    of_base = mirror.at[:, 0].set(jnp.where(is_first, first_base, mirror[:, 0]))
    of_mirror = base.at[:, 0].set(jnp.where(is_first, first_mirror, base[:, 0]))
    return of_base, of_mirror


def post_process(spec, partner, turn):
    even = 0.5 * (spec + partner)
    odd = jnp.stack([0.5 * (spec[1] - partner[1]), -0.5 * (spec[0] - partner[0])])
    return even + complex_mul(odd, turn)


def pre_process(filtered, partner, turn):
    even_back = 0.5 * (filtered + partner)
    odd_back = complex_mul(0.5 * (filtered - partner), conjugate(turn))
    return jnp.stack([even_back[0] - odd_back[1], even_back[1] + odd_back[0]])


def middle_kernel(spec_ref, phase_ref, row_ref, column_ref, out_ref):
    turn_re = row_ref[0] * column_ref[0] - row_ref[1] * column_ref[1]
    turn_im = row_ref[0] * column_ref[1] + row_ref[1] * column_ref[0]
    filtered = []
    for half in (0, 1):
        other = 1 - half
        spec = jnp.stack([spec_ref[0, half], spec_ref[1, half]])
        partner = jnp.stack([spec_ref[0, other], -spec_ref[1, other]])
        turn = jnp.stack([turn_re[half], turn_im[half]])
        transformed = post_process(spec, partner, turn)
        phase = phase_ref[half]
        filtered.append(complex_mul(transformed, jnp.stack([jnp.cos(phase), jnp.sin(phase)])))
    for half in (0, 1):
        other = filtered[1 - half]
        turn = jnp.stack([turn_re[half], turn_im[half]])
        packed = pre_process(filtered[half], conjugate(other), turn)
        out_ref[0, half] = packed[0]
        out_ref[1, half] = packed[1]


def middle(spectrum, phase_rows, row_turn, column_turn):
    rows = spectrum.shape[2]
    columns = spectrum.shape[3]
    spec_block = pl.BlockSpec((2, 2, TILE_ROWS, columns), lambda i: (0, 0, i, 0))
    return pl.pallas_call(
        middle_kernel,
        out_shape=jax.ShapeDtypeStruct(spectrum.shape, jnp.float32),
        grid=(rows // TILE_ROWS,),
        in_specs=[
            spec_block,
            pl.BlockSpec((2, TILE_ROWS, columns), lambda i: (0, i, 0)),
            pl.BlockSpec((2, 2, TILE_ROWS, 1), lambda i: (0, 0, i, 0)),
            pl.BlockSpec((2, 2, 1, columns), lambda i: (0, 0, 0, 0)),
        ],
        out_specs=spec_block,
    )(spectrum, phase_rows, row_turn, column_turn)


def per_device(voltage, chirp_phase):
    groups = lax.axis_size("fft")
    device = lax.axis_index("fft")
    quarter = voltage.shape[2]
    row_count = 4 * quarter
    local_width = voltage.shape[3]
    columns = local_width * groups
    second_len = columns // B1
    total_bins = row_count * columns
    half_count = row_count // (2 * groups)
    local_rows = 2 * half_count
    is_first = device == 0
    row_order = fold_order(row_count, groups)
    local_order = lax.dynamic_slice_in_dim(row_order, device * local_rows, local_rows)
    first_range = jnp.arange(B1, dtype=jnp.int32)
    second_range = jnp.arange(second_len, dtype=jnp.int32)
    column_range = jnp.arange(columns, dtype=jnp.int32)
    sample_rows = jnp.arange(quarter, dtype=jnp.int32)
    entry_table = real_table(rotation(sample_rows[:, None] * row_order[None, :], row_count))
    device_turn = rotation(row_order * (device * local_width), total_bins)
    block_range = jnp.arange(B1 // groups, dtype=jnp.int32)
    within_turn = rotation(row_order[:, None] * (second_len * block_range)[None, :], total_bins)
    inner_turn = rotation(row_order[:, None] * second_range[None, :], total_bins)
    outer_turn = complex_mul(device_turn[:, :, None], within_turn)
    section_one = both_halves(first_range, first_range, B1, False, True)
    block_turn = both_halves(first_range, second_range, columns, True, False)
    section_two = both_halves(second_range, second_range, second_len, False, True)
    samples_in = voltage[0].reshape(2, quarter, B1 // groups, second_len)
    piece = second_len // CHUNKS
    spectrum = None
    for chunk in range(CHUNKS):
        cut = slice(chunk * piece, (chunk + 1) * piece)
        spread = jnp.einsum("pmun,pqmr->qrun", samples_in[..., cut], entry_table, precision=HIGHEST)
        spread = complex_mul(complex_mul(spread, outer_turn[..., None]), inner_turn[:, :, None, cut])
        gathered = lax.all_to_all(spread, "fft", split_axis=1, concat_axis=2, tiled=True)
        gathered = gathered.reshape(2, 2, half_count, B1, piece)
        gathered = jnp.einsum(
            "phrun,pqhuk->qhrkn", gathered, real_table(section_one), precision=HIGHEST
        )
        gathered = complex_mul(gathered, block_turn[:, :, None, :, cut])
        part = jnp.einsum(
            "phrkn,pqhnj->qhrjk", gathered, real_table(section_two[:, :, cut]), precision=HIGHEST
        )
        spectrum = part if spectrum is None else spectrum + part
    spectrum = spectrum.reshape(2, 2, half_count, columns)
    half_rows = jnp.stack([local_order[:half_count], local_order[half_count:]])
    row_turn = rotation(half_rows, 2 * total_bins)[..., None]
    stored_columns = jnp.stack([column_range, columns - 1 - column_range])
    column_turn = rotation(stored_columns, 2 * columns)[:, :, None, :]
    phase_rows = jnp.stack([chirp_phase[0], reverse_lanes(chirp_phase[1])])
    packed = middle(spectrum, phase_rows, row_turn, column_turn)
    first_spec = spectrum[:, :, 0]
    first_turn = complex_mul(row_turn[:, :, 0], column_turn[:, :, 0])
    live = jnp.stack([column_range > 0, column_range >= 0])
    first_partner = jnp.stack(
        [jnp.roll(reverse_lanes(first_spec[:, 0]), 1, axis=-1), reverse_lanes(first_spec[:, 1])], axis=1
    )
    first_filtered = complex_mul(
        post_process(first_spec, conjugate(first_partner), first_turn),
        jnp.stack([jnp.cos(phase_rows[:, 0]), jnp.sin(phase_rows[:, 0])]),
    )
    first_filtered = jnp.where(live[None], first_filtered, 0.0)
    first_partner = jnp.stack(
        [jnp.roll(reverse_lanes(first_filtered[:, 0]), 1, axis=-1), reverse_lanes(first_filtered[:, 1])],
        axis=1,
    )
    first_packed = pre_process(first_filtered, conjugate(first_partner), first_turn)
    packed = packed.at[:, :, 0].set(jnp.where(is_first, first_packed, packed[:, :, 0]))
    packed = packed.reshape(2, 2, half_count, second_len, B1)
    back_two = both_halves(second_range, second_range, second_len, True, False)
    back_turn = both_halves(first_range, second_range, columns, True, False)
    back_one = both_halves(first_range, first_range, B1, True, False)
    upper_turn = rotation(local_order[:, None] * (second_len * first_range)[None, :], total_bins)
    lower_turn = rotation(local_order[:, None] * second_range[None, :], total_bins)
    exit_turn = rotation(
        row_order[:, None] * jnp.arange(row_count, dtype=jnp.int32)[None, :], row_count
    )
    exit_table = real_table(jnp.stack([exit_turn[0] / total_bins, -exit_turn[1] / total_bins]))
    outputs = []
    for chunk in range(CHUNKS):
        cut = slice(chunk * piece, (chunk + 1) * piece)
        signal = jnp.einsum(
            "phrjk,pqhjv->qhrkv", packed, real_table(conjugate(back_two[:, :, :, cut])), precision=HIGHEST
        )
        signal = complex_mul(signal, conjugate(back_turn[:, :, :, cut])[:, :, None])
        signal = jnp.einsum(
            "phrkv,pqhku->qhruv", signal, real_table(conjugate(back_one)), precision=HIGHEST
        )
        signal = signal.reshape(2, local_rows, B1, piece)
        signal = complex_mul(
            complex_mul(signal, conjugate(upper_turn)[..., None]),
            conjugate(lower_turn[:, :, cut])[:, :, None, :],
        )
        signal = signal.reshape(2, local_rows, groups, B1 // groups, piece)
        arrived = lax.all_to_all(signal, "fft", split_axis=2, concat_axis=1, tiled=True)
        arrived = arrived.reshape(2, row_count, B1 // groups, piece)

        def sample_block(block_id):
            lower = block_id * quarter
            table = exit_table[:, :, :, lower : lower + quarter]
            return jnp.einsum("prun,pqrm->qmun", arrived, table, precision=HIGHEST)

        running = sample_block(3)
        for block_id in (2, 1, 0):
            running = sample_block(block_id) + passed_along(running, "seg", 1)
        outputs.append(running)
    running = jnp.concatenate(outputs, axis=-1).reshape(2, quarter, local_width)
    return running[None]


def solution(mesh):
    in_specs = (P("seg", None, None, "fft"), P(None, "fft", None))
    out_specs = P("seg", None, None, "fft")
    return jax.shard_map(
        per_device, mesh=mesh, in_specs=in_specs, out_specs=out_specs, check_vma=False
    )
```

```python
import math

import jax
import jax.numpy as jnp
from jax import lax
from jax.experimental import pallas as pl
from jax.sharding import PartitionSpec as P

B1 = 64
TILE_ROWS = 8


HIGHEST = lax.Precision.HIGHEST
HIGH = lax.Precision.HIGH


def passed_along(shard, axis, by):
    length = lax.axis_size(axis)
    pairs = [(i, i + by) for i in range(length) if 0 <= i + by < length]
    return lax.ppermute(shard, axis, pairs)


def rotation(products, period):
    reduced = jnp.mod(products, period).astype(jnp.float32)
    angles = reduced * jnp.float32(-2.0 * math.pi / period)
    return jnp.stack([jnp.cos(angles), jnp.sin(angles)])


def conjugate(pair):
    return jnp.stack([pair[0], -pair[1]])


def real_table(pair):
    return jnp.stack([jnp.stack([pair[0], pair[1]]), jnp.stack([-pair[1], pair[0]])])


def complex_mul(left_pair, right_pair):
    first = left_pair[0] * right_pair[0] - left_pair[1] * right_pair[1]
    second = left_pair[0] * right_pair[1] + left_pair[1] * right_pair[0]
    return jnp.stack([first, second])


def fold_order(row_count, groups):
    half_count = row_count // (2 * groups)
    places = jnp.arange(row_count, dtype=jnp.int32)
    within = places % (2 * half_count)
    base_row = places // (2 * half_count) * half_count + within % half_count
    mirror_row = jnp.where(base_row > 0, row_count - base_row, row_count // 2)
    return jnp.where(within >= half_count, mirror_row, base_row)


def both_halves(outer, inner, period, reverse_outer, reverse_inner):
    last_outer = outer.shape[0] - 1
    last_inner = inner.shape[0] - 1
    natural = outer[:, None] * inner[None, :]
    outer_turned = (last_outer - outer) if reverse_outer else outer
    inner_turned = (last_inner - inner) if reverse_inner else inner
    turned = outer_turned[:, None] * inner_turned[None, :]
    return jnp.stack([rotation(natural, period), rotation(turned, period)], axis=1)


def reverse_lanes(values):
    width = values.shape[-1]
    tiles = values.reshape(values.shape[:-1] + (width // 128, 128))
    tiles = jnp.flip(tiles, axis=-2)
    lane = jnp.arange(128, dtype=jnp.int32)
    anti = (lane[:, None] + lane[None, :] == 127).astype(jnp.float32)
    flipped = jnp.einsum("...l,lm->...m", tiles, anti, precision=HIGHEST)
    return flipped.reshape(values.shape)


def partners(base, mirror, is_first):
    first_base = jnp.roll(reverse_lanes(base[:, 0]), 1, axis=-1)
    first_mirror = reverse_lanes(mirror[:, 0])
    of_base = mirror.at[:, 0].set(jnp.where(is_first, first_base, mirror[:, 0]))
    of_mirror = base.at[:, 0].set(jnp.where(is_first, first_mirror, base[:, 0]))
    return of_base, of_mirror


def post_process(spec, partner, turn):
    even = 0.5 * (spec + partner)
    odd = jnp.stack([0.5 * (spec[1] - partner[1]), -0.5 * (spec[0] - partner[0])])
    return even + complex_mul(odd, turn)


def pre_process(filtered, partner, turn):
    even_back = 0.5 * (filtered + partner)
    odd_back = complex_mul(0.5 * (filtered - partner), conjugate(turn))
    return jnp.stack([even_back[0] - odd_back[1], even_back[1] + odd_back[0]])


def middle_kernel(spec_ref, phase_ref, row_ref, column_ref, out_ref):
    turn_re = row_ref[0] * column_ref[0] - row_ref[1] * column_ref[1]
    turn_im = row_ref[0] * column_ref[1] + row_ref[1] * column_ref[0]
    filtered = []
    for half in (0, 1):
        other = 1 - half
        spec = jnp.stack([spec_ref[0, half], spec_ref[1, half]])
        partner = jnp.stack([spec_ref[0, other], -spec_ref[1, other]])
        turn = jnp.stack([turn_re[half], turn_im[half]])
        transformed = post_process(spec, partner, turn)
        phase = phase_ref[half]
        filtered.append(complex_mul(transformed, jnp.stack([jnp.cos(phase), jnp.sin(phase)])))
    for half in (0, 1):
        other = filtered[1 - half]
        turn = jnp.stack([turn_re[half], turn_im[half]])
        packed = pre_process(filtered[half], conjugate(other), turn)
        out_ref[0, half] = packed[0]
        out_ref[1, half] = packed[1]


def middle(spectrum, phase_rows, row_turn, column_turn):
    rows = spectrum.shape[2]
    columns = spectrum.shape[3]
    spec_block = pl.BlockSpec((2, 2, TILE_ROWS, columns), lambda i: (0, 0, i, 0))
    return pl.pallas_call(
        middle_kernel,
        out_shape=jax.ShapeDtypeStruct(spectrum.shape, jnp.float32),
        grid=(rows // TILE_ROWS,),
        in_specs=[
            spec_block,
            pl.BlockSpec((2, TILE_ROWS, columns), lambda i: (0, i, 0)),
            pl.BlockSpec((2, 2, TILE_ROWS, 1), lambda i: (0, 0, i, 0)),
            pl.BlockSpec((2, 2, 1, columns), lambda i: (0, 0, 0, 0)),
        ],
        out_specs=spec_block,
    )(spectrum, phase_rows, row_turn, column_turn)


def per_device(voltage, chirp_phase):
    groups = lax.axis_size("fft")
    device = lax.axis_index("fft")
    quarter = voltage.shape[2]
    row_count = 4 * quarter
    local_width = voltage.shape[3]
    columns = local_width * groups
    second_len = columns // B1
    total_bins = row_count * columns
    half_count = row_count // (2 * groups)
    local_rows = 2 * half_count
    is_first = device == 0
    row_order = fold_order(row_count, groups)
    local_order = lax.dynamic_slice_in_dim(row_order, device * local_rows, local_rows)
    first_range = jnp.arange(B1, dtype=jnp.int32)
    second_range = jnp.arange(second_len, dtype=jnp.int32)
    column_range = jnp.arange(columns, dtype=jnp.int32)
    sample_rows = jnp.arange(quarter, dtype=jnp.int32)
    entry_table = real_table(rotation(sample_rows[:, None] * row_order[None, :], row_count))
    spread = jnp.einsum("pmb,pqmr->qrb", voltage[0], entry_table, precision=HIGH)
    spread = spread.reshape(2, row_count, B1 // groups, second_len)
    device_turn = rotation(row_order * (device * local_width), total_bins)
    block_range = jnp.arange(B1 // groups, dtype=jnp.int32)
    within_turn = rotation(row_order[:, None] * (second_len * block_range)[None, :], total_bins)
    inner_turn = rotation(row_order[:, None] * second_range[None, :], total_bins)
    outer_turn = complex_mul(device_turn[:, :, None], within_turn)
    spread = complex_mul(complex_mul(spread, outer_turn[..., None]), inner_turn[:, :, None, :])
    gathered = lax.all_to_all(spread, "fft", split_axis=1, concat_axis=2, tiled=True)
    gathered = gathered.reshape(2, 2, half_count, B1, second_len)
    section_one = both_halves(first_range, first_range, B1, False, True)
    block_turn = both_halves(first_range, second_range, columns, True, False)
    section_two = both_halves(second_range, second_range, second_len, False, True)
    gathered = jnp.einsum("phrun,pqhuk->qhrkn", gathered, real_table(section_one), precision=HIGH)
    gathered = complex_mul(gathered, block_turn[:, :, None])
    spectrum = jnp.einsum("phrkn,pqhnj->qhrjk", gathered, real_table(section_two), precision=HIGH)
    spectrum = spectrum.reshape(2, 2, half_count, columns)
    half_rows = jnp.stack([local_order[:half_count], local_order[half_count:]])
    row_turn = rotation(half_rows, 2 * total_bins)[..., None]
    stored_columns = jnp.stack([column_range, columns - 1 - column_range])
    column_turn = rotation(stored_columns, 2 * columns)[:, :, None, :]
    phase_rows = jnp.stack([chirp_phase[0], reverse_lanes(chirp_phase[1])])
    packed = middle(spectrum, phase_rows, row_turn, column_turn)
    first_spec = spectrum[:, :, 0]
    first_turn = complex_mul(row_turn[:, :, 0], column_turn[:, :, 0])
    live = jnp.stack([column_range > 0, column_range >= 0])
    first_partner = jnp.stack(
        [jnp.roll(reverse_lanes(first_spec[:, 0]), 1, axis=-1), reverse_lanes(first_spec[:, 1])], axis=1
    )
    first_filtered = complex_mul(
        post_process(first_spec, conjugate(first_partner), first_turn),
        jnp.stack([jnp.cos(phase_rows[:, 0]), jnp.sin(phase_rows[:, 0])]),
    )
    first_filtered = jnp.where(live[None], first_filtered, 0.0)
    first_partner = jnp.stack(
        [jnp.roll(reverse_lanes(first_filtered[:, 0]), 1, axis=-1), reverse_lanes(first_filtered[:, 1])],
        axis=1,
    )
    first_packed = pre_process(first_filtered, conjugate(first_partner), first_turn)
    packed = packed.at[:, :, 0].set(jnp.where(is_first, first_packed, packed[:, :, 0]))
    packed = packed.reshape(2, 2, half_count, second_len, B1)
    back_two = both_halves(second_range, second_range, second_len, True, False)
    back_turn = both_halves(first_range, second_range, columns, True, False)
    back_one = both_halves(first_range, first_range, B1, True, False)
    packed = jnp.einsum(
        "phrjk,pqhjv->qhrkv", packed, real_table(conjugate(back_two)), precision=HIGH
    )
    packed = complex_mul(packed, conjugate(back_turn)[:, :, None])
    packed = jnp.einsum(
        "phrkv,pqhku->qhruv", packed, real_table(conjugate(back_one)), precision=HIGH
    )
    packed = packed.reshape(2, local_rows, B1, second_len)
    upper_turn = rotation(local_order[:, None] * (second_len * first_range)[None, :], total_bins)
    lower_turn = rotation(local_order[:, None] * second_range[None, :], total_bins)
    packed = complex_mul(
        complex_mul(packed, conjugate(upper_turn)[..., None]), conjugate(lower_turn)[:, :, None, :]
    )
    packed = packed.reshape(2, local_rows, groups, local_width)
    arrived = lax.all_to_all(packed, "fft", split_axis=2, concat_axis=1, tiled=True)
    arrived = arrived.reshape(2, row_count, local_width)
    exit_turn = rotation(
        row_order[:, None] * jnp.arange(row_count, dtype=jnp.int32)[None, :], row_count
    )
    exit_table = real_table(jnp.stack([exit_turn[0] / total_bins, -exit_turn[1] / total_bins]))

    def sample_block(block_id):
        lower = block_id * quarter
        table = exit_table[:, :, :, lower : lower + quarter]
        return jnp.einsum("prn,pqrm->qmn", arrived, table, precision=HIGH)

    running = sample_block(3)
    for block_id in (2, 1, 0):
        running = sample_block(block_id) + passed_along(running, "seg", 1)
    return running[None]


def solution(mesh):
    in_specs = (P("seg", None, None, "fft"), P(None, "fft", None))
    out_specs = P("seg", None, None, "fft")
    return jax.shard_map(
        per_device, mesh=mesh, in_specs=in_specs, out_specs=out_specs, check_vma=False
    )
```

```python
import math

import jax
import jax.numpy as jnp
from jax import lax
from jax.experimental import pallas as pl
from jax.sharding import PartitionSpec as P

B1 = 64
TILE_ROWS = 8


HIGHEST = lax.Precision.HIGHEST
HIGH = lax.Precision.HIGH


def passed_along(shard, axis, by):
    length = lax.axis_size(axis)
    pairs = [(i, i + by) for i in range(length) if 0 <= i + by < length]
    return lax.ppermute(shard, axis, pairs)


def rotation(products, period):
    reduced = jnp.mod(products, period).astype(jnp.float32)
    angles = reduced * jnp.float32(-2.0 * math.pi / period)
    return jnp.stack([jnp.cos(angles), jnp.sin(angles)])


def conjugate(pair):
    return jnp.stack([pair[0], -pair[1]])


def real_table(pair):
    return jnp.stack([jnp.stack([pair[0], pair[1]]), jnp.stack([-pair[1], pair[0]])])


def complex_mul(left_pair, right_pair):
    first = left_pair[0] * right_pair[0] - left_pair[1] * right_pair[1]
    second = left_pair[0] * right_pair[1] + left_pair[1] * right_pair[0]
    return jnp.stack([first, second])


def fold_order(row_count, groups):
    half_count = row_count // (2 * groups)
    places = jnp.arange(row_count, dtype=jnp.int32)
    within = places % (2 * half_count)
    base_row = places // (2 * half_count) * half_count + within % half_count
    mirror_row = jnp.where(base_row > 0, row_count - base_row, row_count // 2)
    return jnp.where(within >= half_count, mirror_row, base_row)


def both_halves(outer, inner, period, reverse_outer, reverse_inner):
    last_outer = outer.shape[0] - 1
    last_inner = inner.shape[0] - 1
    natural = outer[:, None] * inner[None, :]
    outer_turned = (last_outer - outer) if reverse_outer else outer
    inner_turned = (last_inner - inner) if reverse_inner else inner
    turned = outer_turned[:, None] * inner_turned[None, :]
    return jnp.stack([rotation(natural, period), rotation(turned, period)], axis=1)


def reverse_lanes(values):
    width = values.shape[-1]
    tiles = values.reshape(values.shape[:-1] + (width // 128, 128))
    tiles = jnp.flip(tiles, axis=-2)
    lane = jnp.arange(128, dtype=jnp.int32)
    anti = (lane[:, None] + lane[None, :] == 127).astype(jnp.float32)
    flipped = jnp.einsum("...l,lm->...m", tiles, anti, precision=HIGHEST)
    return flipped.reshape(values.shape)


def partners(base, mirror, is_first):
    first_base = jnp.roll(reverse_lanes(base[:, 0]), 1, axis=-1)
    first_mirror = reverse_lanes(mirror[:, 0])
    of_base = mirror.at[:, 0].set(jnp.where(is_first, first_base, mirror[:, 0]))
    of_mirror = base.at[:, 0].set(jnp.where(is_first, first_mirror, base[:, 0]))
    return of_base, of_mirror


def post_process(spec, partner, turn):
    even = 0.5 * (spec + partner)
    odd = jnp.stack([0.5 * (spec[1] - partner[1]), -0.5 * (spec[0] - partner[0])])
    return even + complex_mul(odd, turn)


def pre_process(filtered, partner, turn):
    even_back = 0.5 * (filtered + partner)
    odd_back = complex_mul(0.5 * (filtered - partner), conjugate(turn))
    return jnp.stack([even_back[0] - odd_back[1], even_back[1] + odd_back[0]])


def middle_kernel(spec_ref, phase_ref, row_ref, column_ref, out_ref):
    turn_re = row_ref[0] * column_ref[0] - row_ref[1] * column_ref[1]
    turn_im = row_ref[0] * column_ref[1] + row_ref[1] * column_ref[0]
    filtered = []
    for half in (0, 1):
        other = 1 - half
        spec = jnp.stack([spec_ref[0, half], spec_ref[1, half]])
        partner = jnp.stack([spec_ref[0, other], -spec_ref[1, other]])
        turn = jnp.stack([turn_re[half], turn_im[half]])
        transformed = post_process(spec, partner, turn)
        phase = phase_ref[half]
        filtered.append(complex_mul(transformed, jnp.stack([jnp.cos(phase), jnp.sin(phase)])))
    for half in (0, 1):
        other = filtered[1 - half]
        turn = jnp.stack([turn_re[half], turn_im[half]])
        packed = pre_process(filtered[half], conjugate(other), turn)
        out_ref[0, half] = packed[0]
        out_ref[1, half] = packed[1]


def middle(spectrum, phase_rows, row_turn, column_turn):
    rows = spectrum.shape[2]
    columns = spectrum.shape[3]
    spec_block = pl.BlockSpec((2, 2, TILE_ROWS, columns), lambda i: (0, 0, i, 0))
    return pl.pallas_call(
        middle_kernel,
        out_shape=jax.ShapeDtypeStruct(spectrum.shape, jnp.float32),
        grid=(rows // TILE_ROWS,),
        in_specs=[
            spec_block,
            pl.BlockSpec((2, TILE_ROWS, columns), lambda i: (0, i, 0)),
            pl.BlockSpec((2, 2, TILE_ROWS, 1), lambda i: (0, 0, i, 0)),
            pl.BlockSpec((2, 2, 1, columns), lambda i: (0, 0, 0, 0)),
        ],
        out_specs=spec_block,
    )(spectrum, phase_rows, row_turn, column_turn)


def per_device(voltage, chirp_phase):
    groups = lax.axis_size("fft")
    device = lax.axis_index("fft")
    quarter = voltage.shape[2]
    row_count = 4 * quarter
    local_width = voltage.shape[3]
    columns = local_width * groups
    second_len = columns // B1
    total_bins = row_count * columns
    half_count = row_count // (2 * groups)
    local_rows = 2 * half_count
    is_first = device == 0
    row_order = fold_order(row_count, groups)
    local_order = lax.dynamic_slice_in_dim(row_order, device * local_rows, local_rows)
    first_range = jnp.arange(B1, dtype=jnp.int32)
    second_range = jnp.arange(second_len, dtype=jnp.int32)
    column_range = jnp.arange(columns, dtype=jnp.int32)
    sample_rows = jnp.arange(quarter, dtype=jnp.int32)
    entry_table = real_table(rotation(sample_rows[:, None] * row_order[None, :], row_count))
    samples_in = voltage[0].reshape(2, quarter, B1 // groups, second_len)
    entry_blocks = entry_table.reshape(2, 2, quarter, groups, local_rows)
    device_turn = rotation(row_order * (device * local_width), total_bins)
    block_range = jnp.arange(B1 // groups, dtype=jnp.int32)
    within_turn = rotation(row_order[:, None] * (second_len * block_range)[None, :], total_bins)
    inner_turn = rotation(row_order[:, None] * second_range[None, :], total_bins)
    outer_turn = complex_mul(device_turn[:, :, None], within_turn)
    turn = complex_mul(outer_turn[..., None], inner_turn[:, :, None, :])
    turn = turn.reshape(2, groups, local_rows, B1 // groups, second_len)
    spread = jnp.einsum("pmun,pqmdr->dqrun", samples_in, entry_blocks, precision=HIGH)
    spread = jnp.stack([
        spread[:, 0] * turn[0] - spread[:, 1] * turn[1],
        spread[:, 0] * turn[1] + spread[:, 1] * turn[0],
    ], axis=1)
    gathered = lax.all_to_all(spread, "fft", split_axis=0, concat_axis=0, tiled=True)
    gathered = gathered.reshape(groups, 2, 2, half_count, B1 // groups, second_len)
    section_one = both_halves(first_range, first_range, B1, False, True)
    block_turn = both_halves(first_range, second_range, columns, True, False)
    section_two = both_halves(second_range, second_range, second_len, False, True)
    first_blocks = real_table(section_one).reshape(2, 2, 2, groups, B1 // groups, B1)
    gathered = jnp.einsum("sphrun,pqhsuk->qhrkn", gathered, first_blocks, precision=HIGH)
    gathered = complex_mul(gathered, block_turn[:, :, None])
    spectrum = jnp.einsum("phrkn,pqhnj->qhrjk", gathered, real_table(section_two), precision=HIGH)
    spectrum = spectrum.reshape(2, 2, half_count, columns)
    half_rows = jnp.stack([local_order[:half_count], local_order[half_count:]])
    row_turn = rotation(half_rows, 2 * total_bins)[..., None]
    stored_columns = jnp.stack([column_range, columns - 1 - column_range])
    column_turn = rotation(stored_columns, 2 * columns)[:, :, None, :]
    phase_rows = jnp.stack([chirp_phase[0], reverse_lanes(chirp_phase[1])])
    packed = middle(spectrum, phase_rows, row_turn, column_turn)
    first_spec = spectrum[:, :, 0]
    first_turn = complex_mul(row_turn[:, :, 0], column_turn[:, :, 0])
    live = jnp.stack([column_range > 0, column_range >= 0])
    first_partner = jnp.stack(
        [jnp.roll(reverse_lanes(first_spec[:, 0]), 1, axis=-1), reverse_lanes(first_spec[:, 1])], axis=1
    )
    first_filtered = complex_mul(
        post_process(first_spec, conjugate(first_partner), first_turn),
        jnp.stack([jnp.cos(phase_rows[:, 0]), jnp.sin(phase_rows[:, 0])]),
    )
    first_filtered = jnp.where(live[None], first_filtered, 0.0)
    first_partner = jnp.stack(
        [jnp.roll(reverse_lanes(first_filtered[:, 0]), 1, axis=-1), reverse_lanes(first_filtered[:, 1])],
        axis=1,
    )
    first_packed = pre_process(first_filtered, conjugate(first_partner), first_turn)
    packed = packed.at[:, :, 0].set(jnp.where(is_first, first_packed, packed[:, :, 0]))
    packed = packed.reshape(2, 2, half_count, second_len, B1)
    back_two = both_halves(second_range, second_range, second_len, True, False)
    back_turn = both_halves(first_range, second_range, columns, True, False)
    back_one = both_halves(first_range, first_range, B1, True, False)
    packed = jnp.einsum(
        "phrjk,pqhjv->qhrkv", packed, real_table(conjugate(back_two)), precision=HIGH
    )
    packed = complex_mul(packed, conjugate(back_turn)[:, :, None])
    packed = jnp.einsum(
        "phrkv,pqhku->qhruv", packed, real_table(conjugate(back_one)), precision=HIGH
    )
    packed = packed.reshape(2, local_rows, B1, second_len)
    upper_turn = rotation(local_order[:, None] * (second_len * first_range)[None, :], total_bins)
    lower_turn = rotation(local_order[:, None] * second_range[None, :], total_bins)
    packed = complex_mul(
        complex_mul(packed, conjugate(upper_turn)[..., None]), conjugate(lower_turn)[:, :, None, :]
    )
    packed = packed.reshape(2, local_rows, groups, local_width)
    packed = jnp.transpose(packed, (2, 0, 1, 3))
    arrived = lax.all_to_all(packed, "fft", split_axis=0, concat_axis=0, tiled=True)
    exit_turn = rotation(
        row_order[:, None] * jnp.arange(row_count, dtype=jnp.int32)[None, :], row_count
    )
    exit_table = real_table(jnp.stack([exit_turn[0] / total_bins, -exit_turn[1] / total_bins]))

    def sample_block(block_id):
        lower = block_id * quarter
        table = exit_table[:, :, :, lower : lower + quarter]
        table = table.reshape(2, 2, groups, local_rows, quarter)
        return jnp.einsum("sprn,pqsrm->qmn", arrived, table, precision=HIGH)

    running = sample_block(3)
    for block_id in (2, 1, 0):
        running = sample_block(block_id) + passed_along(running, "seg", 1)
    return running[None]


def solution(mesh):
    in_specs = (P("seg", None, None, "fft"), P(None, "fft", None))
    out_specs = P("seg", None, None, "fft")
    return jax.shard_map(
        per_device, mesh=mesh, in_specs=in_specs, out_specs=out_specs, check_vma=False
    )
```

```python
import math

import jax
import jax.numpy as jnp
from jax import lax
from jax.experimental import pallas as pl
from jax.sharding import PartitionSpec as P

B1 = 64
TILE_ROWS = 8


HIGHEST = lax.Precision.HIGHEST
HIGH = lax.Precision.HIGH


def passed_along(shard, axis, by):
    length = lax.axis_size(axis)
    pairs = [(i, i + by) for i in range(length) if 0 <= i + by < length]
    return lax.ppermute(shard, axis, pairs)


def rotation(products, period):
    reduced = jnp.mod(products, period).astype(jnp.float32)
    angles = reduced * jnp.float32(-2.0 * math.pi / period)
    return jnp.stack([jnp.cos(angles), jnp.sin(angles)])


def conjugate(pair):
    return jnp.stack([pair[0], -pair[1]])


def real_table(pair):
    return jnp.stack([jnp.stack([pair[0], pair[1]]), jnp.stack([-pair[1], pair[0]])])


def complex_mul(left_pair, right_pair):
    first = left_pair[0] * right_pair[0] - left_pair[1] * right_pair[1]
    second = left_pair[0] * right_pair[1] + left_pair[1] * right_pair[0]
    return jnp.stack([first, second])


def fold_order(row_count, groups):
    half_count = row_count // (2 * groups)
    places = jnp.arange(row_count, dtype=jnp.int32)
    within = places % (2 * half_count)
    base_row = places // (2 * half_count) * half_count + within % half_count
    mirror_row = jnp.where(base_row > 0, row_count - base_row, row_count // 2)
    return jnp.where(within >= half_count, mirror_row, base_row)


def both_halves(outer, inner, period, reverse_outer, reverse_inner):
    last_outer = outer.shape[0] - 1
    last_inner = inner.shape[0] - 1
    natural = outer[:, None] * inner[None, :]
    outer_turned = (last_outer - outer) if reverse_outer else outer
    inner_turned = (last_inner - inner) if reverse_inner else inner
    turned = outer_turned[:, None] * inner_turned[None, :]
    return jnp.stack([rotation(natural, period), rotation(turned, period)], axis=1)


def reverse_lanes(values):
    width = values.shape[-1]
    tiles = values.reshape(values.shape[:-1] + (width // 128, 128))
    tiles = jnp.flip(tiles, axis=-2)
    lane = jnp.arange(128, dtype=jnp.int32)
    anti = (lane[:, None] + lane[None, :] == 127).astype(jnp.float32)
    flipped = jnp.einsum("...l,lm->...m", tiles, anti, precision=HIGHEST)
    return flipped.reshape(values.shape)


def partners(base, mirror, is_first):
    first_base = jnp.roll(reverse_lanes(base[:, 0]), 1, axis=-1)
    first_mirror = reverse_lanes(mirror[:, 0])
    of_base = mirror.at[:, 0].set(jnp.where(is_first, first_base, mirror[:, 0]))
    of_mirror = base.at[:, 0].set(jnp.where(is_first, first_mirror, base[:, 0]))
    return of_base, of_mirror


def post_process(spec, partner, turn):
    even = 0.5 * (spec + partner)
    odd = jnp.stack([0.5 * (spec[1] - partner[1]), -0.5 * (spec[0] - partner[0])])
    return even + complex_mul(odd, turn)


def pre_process(filtered, partner, turn):
    even_back = 0.5 * (filtered + partner)
    odd_back = complex_mul(0.5 * (filtered - partner), conjugate(turn))
    return jnp.stack([even_back[0] - odd_back[1], even_back[1] + odd_back[0]])


def middle_kernel(spec_ref, phase_ref, row_ref, column_ref, out_ref):
    turn_re = row_ref[0] * column_ref[0] - row_ref[1] * column_ref[1]
    turn_im = row_ref[0] * column_ref[1] + row_ref[1] * column_ref[0]
    filtered = []
    for half in (0, 1):
        other = 1 - half
        spec = jnp.stack([spec_ref[0, half], spec_ref[1, half]])
        partner = jnp.stack([spec_ref[0, other], -spec_ref[1, other]])
        turn = jnp.stack([turn_re[half], turn_im[half]])
        transformed = post_process(spec, partner, turn)
        phase = phase_ref[half]
        filtered.append(complex_mul(transformed, jnp.stack([jnp.cos(phase), jnp.sin(phase)])))
    for half in (0, 1):
        other = filtered[1 - half]
        turn = jnp.stack([turn_re[half], turn_im[half]])
        packed = pre_process(filtered[half], conjugate(other), turn)
        out_ref[0, half] = packed[0]
        out_ref[1, half] = packed[1]


def middle(spectrum, phase_rows, row_turn, column_turn):
    rows = spectrum.shape[2]
    columns = spectrum.shape[3]
    spec_block = pl.BlockSpec((2, 2, TILE_ROWS, columns), lambda i: (0, 0, i, 0))
    return pl.pallas_call(
        middle_kernel,
        out_shape=jax.ShapeDtypeStruct(spectrum.shape, jnp.float32),
        grid=(rows // TILE_ROWS,),
        in_specs=[
            spec_block,
            pl.BlockSpec((2, TILE_ROWS, columns), lambda i: (0, i, 0)),
            pl.BlockSpec((2, 2, TILE_ROWS, 1), lambda i: (0, 0, i, 0)),
            pl.BlockSpec((2, 2, 1, columns), lambda i: (0, 0, 0, 0)),
        ],
        out_specs=spec_block,
    )(spectrum, phase_rows, row_turn, column_turn)


def per_device(voltage, chirp_phase):
    groups = lax.axis_size("fft")
    device = lax.axis_index("fft")
    quarter = voltage.shape[2]
    row_count = 4 * quarter
    local_width = voltage.shape[3]
    columns = local_width * groups
    second_len = columns // B1
    total_bins = row_count * columns
    half_count = row_count // (2 * groups)
    local_rows = 2 * half_count
    is_first = device == 0
    row_order = fold_order(row_count, groups)
    local_order = lax.dynamic_slice_in_dim(row_order, device * local_rows, local_rows)
    first_range = jnp.arange(B1, dtype=jnp.int32)
    second_range = jnp.arange(second_len, dtype=jnp.int32)
    column_range = jnp.arange(columns, dtype=jnp.int32)
    sample_rows = jnp.arange(quarter, dtype=jnp.int32)
    entry_table = real_table(rotation(sample_rows[:, None] * row_order[None, :], row_count))
    samples_in = voltage[0].reshape(2, quarter, B1 // groups, second_len)
    entry_blocks = entry_table.reshape(2, 2, quarter, groups, local_rows)
    device_turn = rotation(row_order * (device * local_width), total_bins)
    block_range = jnp.arange(B1 // groups, dtype=jnp.int32)
    within_turn = rotation(row_order[:, None] * (second_len * block_range)[None, :], total_bins)
    inner_turn = rotation(row_order[:, None] * second_range[None, :], total_bins)
    outer_turn = complex_mul(device_turn[:, :, None], within_turn)
    turn = complex_mul(outer_turn[..., None], inner_turn[:, :, None, :])
    turn = turn.reshape(2, groups, local_rows, B1 // groups, second_len)
    spread = jnp.einsum("pmun,pqmdr->dqrun", samples_in, entry_blocks, precision=HIGH)
    spread = jnp.stack([
        spread[:, 0] * turn[0] - spread[:, 1] * turn[1],
        spread[:, 0] * turn[1] + spread[:, 1] * turn[0],
    ], axis=1)
    gathered = lax.all_to_all(spread, "fft", split_axis=0, concat_axis=0, tiled=True)
    gathered = gathered.reshape(groups, 2, 2, half_count, B1 // groups, second_len)
    section_one = both_halves(first_range, first_range, B1, False, True)
    block_turn = both_halves(first_range, second_range, columns, True, False)
    section_two = both_halves(second_range, second_range, second_len, False, True)
    first_blocks = real_table(section_one).reshape(2, 2, 2, groups, B1 // groups, B1)
    gathered = jnp.einsum("sphrun,pqhsuk->qhrkn", gathered, first_blocks, precision=HIGH)
    gathered = complex_mul(gathered, block_turn[:, :, None])
    spectrum = jnp.einsum("phrkn,pqhnj->qhrjk", gathered, real_table(section_two), precision=HIGH)
    spectrum = spectrum.reshape(2, 2, half_count, columns)
    half_rows = jnp.stack([local_order[:half_count], local_order[half_count:]])
    row_turn = rotation(half_rows, 2 * total_bins)[..., None]
    stored_columns = jnp.stack([column_range, columns - 1 - column_range])
    column_turn = rotation(stored_columns, 2 * columns)[:, :, None, :]
    phase_rows = jnp.stack([chirp_phase[0], reverse_lanes(chirp_phase[1])])
    packed = middle(spectrum, phase_rows, row_turn, column_turn)
    first_spec = spectrum[:, :, 0]
    first_turn = complex_mul(row_turn[:, :, 0], column_turn[:, :, 0])
    live = jnp.stack([column_range > 0, column_range >= 0])
    first_partner = jnp.stack(
        [jnp.roll(reverse_lanes(first_spec[:, 0]), 1, axis=-1), reverse_lanes(first_spec[:, 1])], axis=1
    )
    first_filtered = complex_mul(
        post_process(first_spec, conjugate(first_partner), first_turn),
        jnp.stack([jnp.cos(phase_rows[:, 0]), jnp.sin(phase_rows[:, 0])]),
    )
    first_filtered = jnp.where(live[None], first_filtered, 0.0)
    first_partner = jnp.stack(
        [jnp.roll(reverse_lanes(first_filtered[:, 0]), 1, axis=-1), reverse_lanes(first_filtered[:, 1])],
        axis=1,
    )
    first_packed = pre_process(first_filtered, conjugate(first_partner), first_turn)
    packed = packed.at[:, :, 0].set(jnp.where(is_first, first_packed, packed[:, :, 0]))
    packed = packed.reshape(2, 2, half_count, second_len, B1)
    back_two = both_halves(second_range, second_range, second_len, True, False)
    back_turn = both_halves(first_range, second_range, columns, True, False)
    back_one = both_halves(first_range, first_range, B1, True, False)
    packed = jnp.einsum(
        "phrjk,pqhjv->qhrkv", packed, real_table(conjugate(back_two)), precision=HIGH
    )
    packed = complex_mul(packed, conjugate(back_turn)[:, :, None])
    last_table = real_table(conjugate(back_one))
    packed = [
        jnp.einsum("phrkv,phku->hruv", packed, last_table[:, part], precision=HIGH).reshape(
            local_rows, B1, second_len
        )
        for part in (0, 1)
    ]
    upper_turn = rotation(local_order[:, None] * (second_len * first_range)[None, :], total_bins)
    lower_turn = rotation(local_order[:, None] * second_range[None, :], total_bins)
    back_row = complex_mul(upper_turn[..., None], lower_turn[:, :, None, :])
    signal_re = packed[0] * back_row[0] + packed[1] * back_row[1]
    signal_im = packed[1] * back_row[0] - packed[0] * back_row[1]
    signal_re = jnp.transpose(signal_re.reshape(local_rows, groups, local_width), (1, 0, 2))
    signal_im = jnp.transpose(signal_im.reshape(local_rows, groups, local_width), (1, 0, 2))
    packed = jnp.stack([signal_re, signal_im], axis=1)
    arrived = lax.all_to_all(packed, "fft", split_axis=0, concat_axis=0, tiled=True)
    arrived = jnp.transpose(arrived, (1, 0, 2, 3)).reshape(2, row_count, local_width)
    exit_turn = rotation(
        row_order[:, None] * jnp.arange(row_count, dtype=jnp.int32)[None, :], row_count
    )
    exit_table = real_table(jnp.stack([exit_turn[0] / total_bins, -exit_turn[1] / total_bins]))

    def sample_block(block_id):
        lower = block_id * quarter
        table = exit_table[:, :, :, lower : lower + quarter]
        return jnp.einsum("prn,pqrm->qmn", arrived, table, precision=HIGH)

    running = sample_block(3)
    for block_id in (2, 1, 0):
        running = sample_block(block_id) + passed_along(running, "seg", 1)
    return running[None]


def solution(mesh):
    in_specs = (P("seg", None, None, "fft"), P(None, "fft", None))
    out_specs = P("seg", None, None, "fft")
    return jax.shard_map(
        per_device, mesh=mesh, in_specs=in_specs, out_specs=out_specs, check_vma=False
    )
```

```python
import math

import jax
import jax.numpy as jnp
from jax import lax
from jax.experimental import pallas as pl
from jax.experimental.pallas import tpu as pltpu
from jax.sharding import PartitionSpec as P

B1 = 64
TILE_ROWS = 8
TAIL_CHUNKS = 4


HIGHEST = lax.Precision.HIGHEST
HIGH = lax.Precision.HIGH


def passed_along(shard, axis, by):
    length = lax.axis_size(axis)
    pairs = [(i, i + by) for i in range(length) if 0 <= i + by < length]
    return lax.ppermute(shard, axis, pairs)


def rotation(products, period):
    reduced = jnp.mod(products, period).astype(jnp.float32)
    angles = reduced * jnp.float32(-2.0 * math.pi / period)
    return jnp.stack([jnp.cos(angles), jnp.sin(angles)])


def conjugate(pair):
    return jnp.stack([pair[0], -pair[1]])


def real_table(pair):
    return jnp.stack([jnp.stack([pair[0], pair[1]]), jnp.stack([-pair[1], pair[0]])])


def complex_mul(left_pair, right_pair):
    first = left_pair[0] * right_pair[0] - left_pair[1] * right_pair[1]
    second = left_pair[0] * right_pair[1] + left_pair[1] * right_pair[0]
    return jnp.stack([first, second])


def fold_order(row_count, groups):
    half_count = row_count // (2 * groups)
    places = jnp.arange(row_count, dtype=jnp.int32)
    within = places % (2 * half_count)
    base_row = places // (2 * half_count) * half_count + within % half_count
    mirror_row = jnp.where(base_row > 0, row_count - base_row, row_count // 2)
    return jnp.where(within >= half_count, mirror_row, base_row)


def both_halves(outer, inner, period, reverse_outer, reverse_inner):
    last_outer = outer.shape[0] - 1
    last_inner = inner.shape[0] - 1
    natural = outer[:, None] * inner[None, :]
    outer_turned = (last_outer - outer) if reverse_outer else outer
    inner_turned = (last_inner - inner) if reverse_inner else inner
    turned = outer_turned[:, None] * inner_turned[None, :]
    return jnp.stack([rotation(natural, period), rotation(turned, period)], axis=1)


def reverse_lanes(values):
    width = values.shape[-1]
    tiles = values.reshape(values.shape[:-1] + (width // 128, 128))
    tiles = jnp.flip(tiles, axis=-2)
    lane = jnp.arange(128, dtype=jnp.int32)
    anti = (lane[:, None] + lane[None, :] == 127).astype(jnp.float32)
    flipped = jnp.einsum("...l,lm->...m", tiles, anti, precision=HIGHEST)
    return flipped.reshape(values.shape)


def partners(base, mirror, is_first):
    first_base = jnp.roll(reverse_lanes(base[:, 0]), 1, axis=-1)
    first_mirror = reverse_lanes(mirror[:, 0])
    of_base = mirror.at[:, 0].set(jnp.where(is_first, first_base, mirror[:, 0]))
    of_mirror = base.at[:, 0].set(jnp.where(is_first, first_mirror, base[:, 0]))
    return of_base, of_mirror


def post_process(spec, partner, turn):
    even = 0.5 * (spec + partner)
    odd = jnp.stack([0.5 * (spec[1] - partner[1]), -0.5 * (spec[0] - partner[0])])
    return even + complex_mul(odd, turn)


def pre_process(filtered, partner, turn):
    even_back = 0.5 * (filtered + partner)
    odd_back = complex_mul(0.5 * (filtered - partner), conjugate(turn))
    return jnp.stack([even_back[0] - odd_back[1], even_back[1] + odd_back[0]])


def middle_kernel(spec_ref, phase_ref, row_ref, column_ref, out_ref):
    turn_re = row_ref[0] * column_ref[0] - row_ref[1] * column_ref[1]
    turn_im = row_ref[0] * column_ref[1] + row_ref[1] * column_ref[0]
    filtered = []
    for half in (0, 1):
        other = 1 - half
        spec = jnp.stack([spec_ref[0, half], spec_ref[1, half]])
        partner = jnp.stack([spec_ref[0, other], -spec_ref[1, other]])
        turn = jnp.stack([turn_re[half], turn_im[half]])
        transformed = post_process(spec, partner, turn)
        phase = phase_ref[half]
        filtered.append(complex_mul(transformed, jnp.stack([jnp.cos(phase), jnp.sin(phase)])))
    for half in (0, 1):
        other = filtered[1 - half]
        turn = jnp.stack([turn_re[half], turn_im[half]])
        packed = pre_process(filtered[half], conjugate(other), turn)
        out_ref[0, half] = packed[0]
        out_ref[1, half] = packed[1]


def middle(spectrum, phase_rows, row_turn, column_turn):
    rows = spectrum.shape[2]
    columns = spectrum.shape[3]
    spec_block = pl.BlockSpec((2, 2, TILE_ROWS, columns), lambda i: (0, 0, i, 0))
    return pl.pallas_call(
        middle_kernel,
        out_shape=jax.ShapeDtypeStruct(spectrum.shape, jnp.float32),
        grid=(rows // TILE_ROWS,),
        in_specs=[
            spec_block,
            pl.BlockSpec((2, TILE_ROWS, columns), lambda i: (0, i, 0)),
            pl.BlockSpec((2, 2, TILE_ROWS, 1), lambda i: (0, 0, i, 0)),
            pl.BlockSpec((2, 2, 1, columns), lambda i: (0, 0, 0, 0)),
        ],
        out_specs=spec_block,
    )(spectrum, phase_rows, row_turn, column_turn)


def tail_kernel(b1_ref, b2_ref, b3_ref, out_ref, land, sums, send_sem, recv_sem):
    me = lax.axis_index("seg")
    count = lax.axis_size("seg")
    lane = lax.axis_index("fft")
    right = lax.rem(me + 1, count)
    left = lax.rem(me + count - 1, count)
    rows = b1_ref.shape[1] // TAIL_CHUNKS
    barrier = pltpu.get_barrier_semaphore()
    for neighbour in (left, right):
        pl.semaphore_signal(
            barrier, inc=1, device_id=(neighbour, lane), device_id_type=pl.DeviceIdType.MESH
        )
    pl.semaphore_wait(barrier, 2)
    keep = jnp.where(me > 0, 1.0, 0.0).astype(jnp.float32)

    def hop(step, chunk, source):
        part = pl.ds(chunk * rows, rows)
        return pltpu.make_async_remote_copy(
            src_ref=source.at[:, part],
            dst_ref=land.at[step, :, part],
            send_sem=send_sem.at[step, chunk],
            recv_sem=recv_sem.at[step, chunk],
            device_id=(right, lane),
            device_id_type=pl.DeviceIdType.MESH,
        )

    copies = []
    for chunk in range(TAIL_CHUNKS):
        copy = hop(0, chunk, b3_ref)
        copy.start()
        copies.append(copy)
    for step, block_ref in ((1, b2_ref), (2, b1_ref)):
        for chunk in range(TAIL_CHUNKS):
            part = pl.ds(chunk * rows, rows)
            copies[(step - 1) * TAIL_CHUNKS + chunk].wait_recv()
            sums[step - 1, :, part] = block_ref[:, part] + keep * land[step - 1, :, part]
            copy = hop(step, chunk, sums.at[step - 1])
            copy.start()
            copies.append(copy)
    for chunk in range(TAIL_CHUNKS):
        part = pl.ds(chunk * rows, rows)
        copies[2 * TAIL_CHUNKS + chunk].wait_recv()
        out_ref[:, part] = keep * land[2, :, part]
    for copy in copies:
        copy.wait_send()


def tail_sum(b1, b2, b3):
    return pl.pallas_call(
        tail_kernel,
        out_shape=jax.ShapeDtypeStruct(b1.shape, jnp.float32),
        in_specs=[pl.BlockSpec(memory_space=pltpu.VMEM)] * 3,
        out_specs=pl.BlockSpec(memory_space=pltpu.VMEM),
        scratch_shapes=[
            pltpu.VMEM((3,) + b1.shape, jnp.float32),
            pltpu.VMEM((2,) + b1.shape, jnp.float32),
            pltpu.SemaphoreType.DMA((3, TAIL_CHUNKS)),
            pltpu.SemaphoreType.DMA((3, TAIL_CHUNKS)),
        ],
        compiler_params=pltpu.CompilerParams(collective_id=0, has_side_effects=True),
    )(b1, b2, b3)


def per_device(voltage, chirp_phase):
    groups = lax.axis_size("fft")
    device = lax.axis_index("fft")
    quarter = voltage.shape[2]
    row_count = 4 * quarter
    local_width = voltage.shape[3]
    columns = local_width * groups
    second_len = columns // B1
    total_bins = row_count * columns
    half_count = row_count // (2 * groups)
    local_rows = 2 * half_count
    is_first = device == 0
    row_order = fold_order(row_count, groups)
    local_order = lax.dynamic_slice_in_dim(row_order, device * local_rows, local_rows)
    first_range = jnp.arange(B1, dtype=jnp.int32)
    second_range = jnp.arange(second_len, dtype=jnp.int32)
    column_range = jnp.arange(columns, dtype=jnp.int32)
    sample_rows = jnp.arange(quarter, dtype=jnp.int32)
    entry_table = real_table(rotation(sample_rows[:, None] * row_order[None, :], row_count))
    samples_in = voltage[0].reshape(2, quarter, B1 // groups, second_len)
    entry_blocks = entry_table.reshape(2, 2, quarter, groups, local_rows)
    device_turn = rotation(row_order * (device * local_width), total_bins)
    block_range = jnp.arange(B1 // groups, dtype=jnp.int32)
    within_turn = rotation(row_order[:, None] * (second_len * block_range)[None, :], total_bins)
    inner_turn = rotation(row_order[:, None] * second_range[None, :], total_bins)
    outer_turn = complex_mul(device_turn[:, :, None], within_turn)
    turn = complex_mul(outer_turn[..., None], inner_turn[:, :, None, :])
    turn = turn.reshape(2, groups, local_rows, B1 // groups, second_len)
    spread = jnp.einsum("pmun,pqmdr->dqrun", samples_in, entry_blocks, precision=HIGH)
    spread = jnp.stack([
        spread[:, 0] * turn[0] - spread[:, 1] * turn[1],
        spread[:, 0] * turn[1] + spread[:, 1] * turn[0],
    ], axis=1)
    gathered = lax.all_to_all(spread, "fft", split_axis=0, concat_axis=0, tiled=True)
    gathered = gathered.reshape(groups, 2, 2, half_count, B1 // groups, second_len)
    section_one = both_halves(first_range, first_range, B1, False, True)
    block_turn = both_halves(first_range, second_range, columns, True, False)
    section_two = both_halves(second_range, second_range, second_len, False, True)
    first_blocks = real_table(section_one).reshape(2, 2, 2, groups, B1 // groups, B1)
    gathered = jnp.einsum("sphrun,pqhsuk->qhrkn", gathered, first_blocks, precision=HIGH)
    gathered = complex_mul(gathered, block_turn[:, :, None])
    spectrum = jnp.einsum("phrkn,pqhnj->qhrjk", gathered, real_table(section_two), precision=HIGH)
    spectrum = spectrum.reshape(2, 2, half_count, columns)
    half_rows = jnp.stack([local_order[:half_count], local_order[half_count:]])
    row_turn = rotation(half_rows, 2 * total_bins)[..., None]
    stored_columns = jnp.stack([column_range, columns - 1 - column_range])
    column_turn = rotation(stored_columns, 2 * columns)[:, :, None, :]
    phase_rows = jnp.stack([chirp_phase[0], reverse_lanes(chirp_phase[1])])
    packed = middle(spectrum, phase_rows, row_turn, column_turn)
    first_spec = spectrum[:, :, 0]
    first_turn = complex_mul(row_turn[:, :, 0], column_turn[:, :, 0])
    live = jnp.stack([column_range > 0, column_range >= 0])
    first_partner = jnp.stack(
        [jnp.roll(reverse_lanes(first_spec[:, 0]), 1, axis=-1), reverse_lanes(first_spec[:, 1])], axis=1
    )
    first_filtered = complex_mul(
        post_process(first_spec, conjugate(first_partner), first_turn),
        jnp.stack([jnp.cos(phase_rows[:, 0]), jnp.sin(phase_rows[:, 0])]),
    )
    first_filtered = jnp.where(live[None], first_filtered, 0.0)
    first_partner = jnp.stack(
        [jnp.roll(reverse_lanes(first_filtered[:, 0]), 1, axis=-1), reverse_lanes(first_filtered[:, 1])],
        axis=1,
    )
    first_packed = pre_process(first_filtered, conjugate(first_partner), first_turn)
    packed = packed.at[:, :, 0].set(jnp.where(is_first, first_packed, packed[:, :, 0]))
    packed = packed.reshape(2, 2, half_count, second_len, B1)
    back_two = both_halves(second_range, second_range, second_len, True, False)
    back_turn = both_halves(first_range, second_range, columns, True, False)
    back_one = both_halves(first_range, first_range, B1, True, False)
    packed = jnp.einsum(
        "phrjk,pqhjv->qhrkv", packed, real_table(conjugate(back_two)), precision=HIGH
    )
    packed = complex_mul(packed, conjugate(back_turn)[:, :, None])
    last_table = real_table(conjugate(back_one))
    packed = [
        jnp.einsum("phrkv,phku->hruv", packed, last_table[:, part], precision=HIGH).reshape(
            local_rows, B1, second_len
        )
        for part in (0, 1)
    ]
    upper_turn = rotation(local_order[:, None] * (second_len * first_range)[None, :], total_bins)
    lower_turn = rotation(local_order[:, None] * second_range[None, :], total_bins)
    back_row = complex_mul(upper_turn[..., None], lower_turn[:, :, None, :])
    signal_re = packed[0] * back_row[0] + packed[1] * back_row[1]
    signal_im = packed[1] * back_row[0] - packed[0] * back_row[1]
    signal_re = jnp.transpose(signal_re.reshape(local_rows, groups, local_width), (1, 0, 2))
    signal_im = jnp.transpose(signal_im.reshape(local_rows, groups, local_width), (1, 0, 2))
    packed = jnp.stack([signal_re, signal_im], axis=1)
    arrived = lax.all_to_all(packed, "fft", split_axis=0, concat_axis=0, tiled=True)
    arrived = jnp.transpose(arrived, (1, 0, 2, 3)).reshape(2, row_count, local_width)
    exit_turn = rotation(
        row_order[:, None] * jnp.arange(row_count, dtype=jnp.int32)[None, :], row_count
    )
    exit_table = real_table(jnp.stack([exit_turn[0] / total_bins, -exit_turn[1] / total_bins]))

    def sample_block(block_id):
        lower = block_id * quarter
        table = exit_table[:, :, :, lower : lower + quarter]
        return jnp.einsum("prn,pqrm->qmn", arrived, table, precision=HIGH)

    tail = tail_sum(sample_block(1), sample_block(2), sample_block(3))
    return (sample_block(0) + tail)[None]


def solution(mesh):
    in_specs = (P("seg", None, None, "fft"), P(None, "fft", None))
    out_specs = P("seg", None, None, "fft")
    return jax.shard_map(
        per_device, mesh=mesh, in_specs=in_specs, out_specs=out_specs, check_vma=False
    )
```

```python
import math

import jax
import jax.numpy as jnp
from jax import lax
from jax.experimental import pallas as pl
from jax.sharding import PartitionSpec as P

B1 = 64
TILE_ROWS = 8


HIGHEST = lax.Precision.HIGHEST
HIGH = lax.Precision.HIGH


def passed_along(shard, axis, by):
    length = lax.axis_size(axis)
    pairs = [(i, i + by) for i in range(length) if 0 <= i + by < length]
    return lax.ppermute(shard, axis, pairs)


def rotation(products, period):
    reduced = jnp.mod(products, period).astype(jnp.float32)
    angles = reduced * jnp.float32(-2.0 * math.pi / period)
    return jnp.stack([jnp.cos(angles), jnp.sin(angles)])


def conjugate(pair):
    return jnp.stack([pair[0], -pair[1]])


def real_table(pair):
    return jnp.stack([jnp.stack([pair[0], pair[1]]), jnp.stack([-pair[1], pair[0]])])


def complex_mul(left_pair, right_pair):
    first = left_pair[0] * right_pair[0] - left_pair[1] * right_pair[1]
    second = left_pair[0] * right_pair[1] + left_pair[1] * right_pair[0]
    return jnp.stack([first, second])


def fold_order(row_count, groups):
    half_count = row_count // (2 * groups)
    places = jnp.arange(row_count, dtype=jnp.int32)
    within = places % (2 * half_count)
    base_row = places // (2 * half_count) * half_count + within % half_count
    mirror_row = jnp.where(base_row > 0, row_count - base_row, row_count // 2)
    return jnp.where(within >= half_count, mirror_row, base_row)


def both_halves(outer, inner, period, reverse_outer, reverse_inner):
    last_outer = outer.shape[0] - 1
    last_inner = inner.shape[0] - 1
    natural = outer[:, None] * inner[None, :]
    outer_turned = (last_outer - outer) if reverse_outer else outer
    inner_turned = (last_inner - inner) if reverse_inner else inner
    turned = outer_turned[:, None] * inner_turned[None, :]
    return jnp.stack([rotation(natural, period), rotation(turned, period)], axis=1)


def reverse_lanes(values):
    width = values.shape[-1]
    tiles = values.reshape(values.shape[:-1] + (width // 128, 128))
    tiles = jnp.flip(tiles, axis=-2)
    lane = jnp.arange(128, dtype=jnp.int32)
    anti = (lane[:, None] + lane[None, :] == 127).astype(jnp.float32)
    flipped = jnp.einsum("...l,lm->...m", tiles, anti, precision=HIGHEST)
    return flipped.reshape(values.shape)


def partners(base, mirror, is_first):
    first_base = jnp.roll(reverse_lanes(base[:, 0]), 1, axis=-1)
    first_mirror = reverse_lanes(mirror[:, 0])
    of_base = mirror.at[:, 0].set(jnp.where(is_first, first_base, mirror[:, 0]))
    of_mirror = base.at[:, 0].set(jnp.where(is_first, first_mirror, base[:, 0]))
    return of_base, of_mirror


def post_process(spec, partner, turn):
    even = 0.5 * (spec + partner)
    odd = jnp.stack([0.5 * (spec[1] - partner[1]), -0.5 * (spec[0] - partner[0])])
    return even + complex_mul(odd, turn)


def pre_process(filtered, partner, turn):
    even_back = 0.5 * (filtered + partner)
    odd_back = complex_mul(0.5 * (filtered - partner), conjugate(turn))
    return jnp.stack([even_back[0] - odd_back[1], even_back[1] + odd_back[0]])


def middle_kernel(spec_ref, phase_ref, row_ref, column_ref, out_ref):
    turn_re = row_ref[0] * column_ref[0] - row_ref[1] * column_ref[1]
    turn_im = row_ref[0] * column_ref[1] + row_ref[1] * column_ref[0]
    filtered = []
    for half in (0, 1):
        other = 1 - half
        spec = jnp.stack([spec_ref[0, half], spec_ref[1, half]])
        partner = jnp.stack([spec_ref[0, other], -spec_ref[1, other]])
        turn = jnp.stack([turn_re[half], turn_im[half]])
        transformed = post_process(spec, partner, turn)
        phase = phase_ref[half]
        filtered.append(complex_mul(transformed, jnp.stack([jnp.cos(phase), jnp.sin(phase)])))
    for half in (0, 1):
        other = filtered[1 - half]
        turn = jnp.stack([turn_re[half], turn_im[half]])
        packed = pre_process(filtered[half], conjugate(other), turn)
        out_ref[0, half] = packed[0]
        out_ref[1, half] = packed[1]


def middle(spectrum, phase_rows, row_turn, column_turn):
    rows = spectrum.shape[2]
    columns = spectrum.shape[3]
    spec_block = pl.BlockSpec((2, 2, TILE_ROWS, columns), lambda i: (0, 0, i, 0))
    return pl.pallas_call(
        middle_kernel,
        out_shape=jax.ShapeDtypeStruct(spectrum.shape, jnp.float32),
        grid=(rows // TILE_ROWS,),
        in_specs=[
            spec_block,
            pl.BlockSpec((2, TILE_ROWS, columns), lambda i: (0, i, 0)),
            pl.BlockSpec((2, 2, TILE_ROWS, 1), lambda i: (0, 0, i, 0)),
            pl.BlockSpec((2, 2, 1, columns), lambda i: (0, 0, 0, 0)),
        ],
        out_specs=spec_block,
    )(spectrum, phase_rows, row_turn, column_turn)


def per_device(voltage, chirp_phase):
    groups = lax.axis_size("fft")
    device = lax.axis_index("fft")
    quarter = voltage.shape[2]
    row_count = 4 * quarter
    local_width = voltage.shape[3]
    columns = local_width * groups
    second_len = columns // B1
    total_bins = row_count * columns
    half_count = row_count // (2 * groups)
    local_rows = 2 * half_count
    is_first = device == 0
    row_order = fold_order(row_count, groups)
    local_order = lax.dynamic_slice_in_dim(row_order, device * local_rows, local_rows)
    first_range = jnp.arange(B1, dtype=jnp.int32)
    second_range = jnp.arange(second_len, dtype=jnp.int32)
    column_range = jnp.arange(columns, dtype=jnp.int32)
    sample_rows = jnp.arange(quarter, dtype=jnp.int32)
    entry_table = real_table(rotation(sample_rows[:, None] * row_order[None, :], row_count))
    samples_in = voltage[0].reshape(2, quarter, B1 // groups, second_len)
    entry_blocks = entry_table.reshape(2, 2, quarter, groups, local_rows)
    device_turn = rotation(row_order * (device * local_width), total_bins)
    block_range = jnp.arange(B1 // groups, dtype=jnp.int32)
    within_turn = rotation(row_order[:, None] * (second_len * block_range)[None, :], total_bins)
    inner_turn = rotation(row_order[:, None] * second_range[None, :], total_bins)
    outer_turn = complex_mul(device_turn[:, :, None], within_turn)
    turn = complex_mul(outer_turn[..., None], inner_turn[:, :, None, :])
    turn = turn.reshape(2, groups, local_rows, B1 // groups, second_len)
    spread = jnp.einsum("pmun,pqmdr->dqrun", samples_in, entry_blocks, precision=HIGH)
    spread = jnp.stack([
        spread[:, 0] * turn[0] - spread[:, 1] * turn[1],
        spread[:, 0] * turn[1] + spread[:, 1] * turn[0],
    ], axis=1)
    gathered = lax.all_to_all(spread, "fft", split_axis=0, concat_axis=0, tiled=True)
    gathered = gathered.reshape(groups, 2, 2, half_count, B1 // groups, second_len)
    section_one = both_halves(first_range, first_range, B1, False, True)
    block_turn = both_halves(first_range, second_range, columns, True, False)
    section_two = both_halves(second_range, second_range, second_len, False, True)
    first_blocks = real_table(section_one).reshape(2, 2, 2, groups, B1 // groups, B1)
    gathered = jnp.einsum("sphrun,pqhsuk->qhrkn", gathered, first_blocks, precision=HIGH)
    gathered = complex_mul(gathered, block_turn[:, :, None])
    spectrum = jnp.einsum("phrkn,pqhnj->qhrjk", gathered, real_table(section_two), precision=HIGH)
    spectrum = spectrum.reshape(2, 2, half_count, columns)
    half_rows = jnp.stack([local_order[:half_count], local_order[half_count:]])
    row_turn = rotation(half_rows, 2 * total_bins)[..., None]
    stored_columns = jnp.stack([column_range, columns - 1 - column_range])
    column_turn = rotation(stored_columns, 2 * columns)[:, :, None, :]
    phase_rows = jnp.stack([chirp_phase[0], reverse_lanes(chirp_phase[1])])
    packed = middle(spectrum, phase_rows, row_turn, column_turn)
    first_spec = spectrum[:, :, 0]
    first_turn = complex_mul(row_turn[:, :, 0], column_turn[:, :, 0])
    live = jnp.stack([column_range > 0, column_range >= 0])
    first_partner = jnp.stack(
        [jnp.roll(reverse_lanes(first_spec[:, 0]), 1, axis=-1), reverse_lanes(first_spec[:, 1])], axis=1
    )
    first_filtered = complex_mul(
        post_process(first_spec, conjugate(first_partner), first_turn),
        jnp.stack([jnp.cos(phase_rows[:, 0]), jnp.sin(phase_rows[:, 0])]),
    )
    first_filtered = jnp.where(live[None], first_filtered, 0.0)
    first_partner = jnp.stack(
        [jnp.roll(reverse_lanes(first_filtered[:, 0]), 1, axis=-1), reverse_lanes(first_filtered[:, 1])],
        axis=1,
    )
    first_packed = pre_process(first_filtered, conjugate(first_partner), first_turn)
    packed = packed.at[:, :, 0].set(jnp.where(is_first, first_packed, packed[:, :, 0]))
    packed = packed.reshape(2, 2, half_count, second_len, B1)
    back_two = both_halves(second_range, second_range, second_len, True, False)
    back_turn = both_halves(first_range, second_range, columns, True, False)
    back_one = both_halves(first_range, first_range, B1, True, False)
    packed = jnp.einsum(
        "phrjk,pqhjv->qhrkv", packed, real_table(conjugate(back_two)), precision=HIGH
    )
    packed = complex_mul(packed, conjugate(back_turn)[:, :, None])
    last_table = real_table(conjugate(back_one))
    packed = [
        jnp.einsum("phrkv,phku->hruv", packed, last_table[:, part], precision=HIGH).reshape(
            local_rows, B1, second_len
        )
        for part in (0, 1)
    ]
    upper_turn = rotation(local_order[:, None] * (second_len * first_range)[None, :], total_bins)
    lower_turn = rotation(local_order[:, None] * second_range[None, :], total_bins)
    back_row = complex_mul(upper_turn[..., None], lower_turn[:, :, None, :])
    signal_re = packed[0] * back_row[0] + packed[1] * back_row[1]
    signal_im = packed[1] * back_row[0] - packed[0] * back_row[1]
    signal_re = jnp.transpose(signal_re.reshape(local_rows, groups, local_width), (1, 0, 2))
    signal_im = jnp.transpose(signal_im.reshape(local_rows, groups, local_width), (1, 0, 2))
    packed = jnp.stack([signal_re, signal_im], axis=1)
    exit_turn = rotation(
        row_order[:, None] * jnp.arange(row_count, dtype=jnp.int32)[None, :], row_count
    )
    exit_table = real_table(jnp.stack([exit_turn[0] / total_bins, -exit_turn[1] / total_bins]))
    piece = local_width // 2
    outputs = []
    for chunk in range(2):
        arrived = lax.all_to_all(
            packed[..., chunk * piece : (chunk + 1) * piece], "fft", split_axis=0, concat_axis=0, tiled=True
        )
        arrived = jnp.transpose(arrived, (1, 0, 2, 3)).reshape(2, row_count, piece)

        def sample_block(block_id):
            lower = block_id * quarter
            table = exit_table[:, :, :, lower : lower + quarter]
            return jnp.einsum("prn,pqrm->qmn", arrived, table, precision=HIGH)

        running = sample_block(3)
        for block_id in (2, 1, 0):
            running = sample_block(block_id) + passed_along(running, "seg", 1)
        outputs.append(running)
    return jnp.concatenate(outputs, axis=-1)[None]


def solution(mesh):
    in_specs = (P("seg", None, None, "fft"), P(None, "fft", None))
    out_specs = P("seg", None, None, "fft")
    return jax.shard_map(
        per_device, mesh=mesh, in_specs=in_specs, out_specs=out_specs, check_vma=False
    )
```

```python
import math

import jax
import jax.numpy as jnp
from jax import lax
from jax.experimental import pallas as pl
from jax.sharding import PartitionSpec as P

B1 = 64
TILE_ROWS = 8


HIGHEST = lax.Precision.HIGHEST
HIGH = lax.Precision.HIGH


def passed_along(shard, axis, by):
    length = lax.axis_size(axis)
    pairs = [(i, i + by) for i in range(length) if 0 <= i + by < length]
    return lax.ppermute(shard, axis, pairs)


def rotation(products, period):
    reduced = jnp.mod(products, period).astype(jnp.float32)
    angles = reduced * jnp.float32(-2.0 * math.pi / period)
    return jnp.stack([jnp.cos(angles), jnp.sin(angles)])


def conjugate(pair):
    return jnp.stack([pair[0], -pair[1]])


def real_table(pair):
    return jnp.stack([jnp.stack([pair[0], pair[1]]), jnp.stack([-pair[1], pair[0]])])


def complex_mul(left_pair, right_pair):
    first = left_pair[0] * right_pair[0] - left_pair[1] * right_pair[1]
    second = left_pair[0] * right_pair[1] + left_pair[1] * right_pair[0]
    return jnp.stack([first, second])


def fold_order(row_count, groups):
    half_count = row_count // (2 * groups)
    places = jnp.arange(row_count, dtype=jnp.int32)
    within = places % (2 * half_count)
    base_row = places // (2 * half_count) * half_count + within % half_count
    mirror_row = jnp.where(base_row > 0, row_count - base_row, row_count // 2)
    return jnp.where(within >= half_count, mirror_row, base_row)


def both_halves(outer, inner, period, reverse_outer, reverse_inner):
    last_outer = outer.shape[0] - 1
    last_inner = inner.shape[0] - 1
    natural = outer[:, None] * inner[None, :]
    outer_turned = (last_outer - outer) if reverse_outer else outer
    inner_turned = (last_inner - inner) if reverse_inner else inner
    turned = outer_turned[:, None] * inner_turned[None, :]
    return jnp.stack([rotation(natural, period), rotation(turned, period)], axis=1)


def reverse_lanes(values):
    width = values.shape[-1]
    tiles = values.reshape(values.shape[:-1] + (width // 128, 128))
    tiles = jnp.flip(tiles, axis=-2)
    lane = jnp.arange(128, dtype=jnp.int32)
    anti = (lane[:, None] + lane[None, :] == 127).astype(jnp.float32)
    flipped = jnp.einsum("...l,lm->...m", tiles, anti, precision=HIGHEST)
    return flipped.reshape(values.shape)


def partners(base, mirror, is_first):
    first_base = jnp.roll(reverse_lanes(base[:, 0]), 1, axis=-1)
    first_mirror = reverse_lanes(mirror[:, 0])
    of_base = mirror.at[:, 0].set(jnp.where(is_first, first_base, mirror[:, 0]))
    of_mirror = base.at[:, 0].set(jnp.where(is_first, first_mirror, base[:, 0]))
    return of_base, of_mirror


def post_process(spec, partner, turn):
    even = 0.5 * (spec + partner)
    odd = jnp.stack([0.5 * (spec[1] - partner[1]), -0.5 * (spec[0] - partner[0])])
    return even + complex_mul(odd, turn)


def pre_process(filtered, partner, turn):
    even_back = 0.5 * (filtered + partner)
    odd_back = complex_mul(0.5 * (filtered - partner), conjugate(turn))
    return jnp.stack([even_back[0] - odd_back[1], even_back[1] + odd_back[0]])


def middle_kernel(spec_ref, cos_ref, sin_ref, row_ref, column_ref, out_ref):
    turn_re = row_ref[0] * column_ref[0] - row_ref[1] * column_ref[1]
    turn_im = row_ref[0] * column_ref[1] + row_ref[1] * column_ref[0]
    filtered = []
    for half in (0, 1):
        other = 1 - half
        spec = jnp.stack([spec_ref[0, half], spec_ref[1, half]])
        partner = jnp.stack([spec_ref[0, other], -spec_ref[1, other]])
        turn = jnp.stack([turn_re[half], turn_im[half]])
        transformed = post_process(spec, partner, turn)
        filtered.append(complex_mul(transformed, jnp.stack([cos_ref[half], sin_ref[half]])))
    for half in (0, 1):
        other = filtered[1 - half]
        turn = jnp.stack([turn_re[half], turn_im[half]])
        packed = pre_process(filtered[half], conjugate(other), turn)
        out_ref[0, half] = packed[0]
        out_ref[1, half] = packed[1]


def middle(spectrum, phase_rows, row_turn, column_turn):
    phase_block = pl.BlockSpec((2, TILE_ROWS, spectrum.shape[3]), lambda i: (0, i, 0))
    rows = spectrum.shape[2]
    columns = spectrum.shape[3]
    spec_block = pl.BlockSpec((2, 2, TILE_ROWS, columns), lambda i: (0, 0, i, 0))
    return pl.pallas_call(
        middle_kernel,
        out_shape=jax.ShapeDtypeStruct(spectrum.shape, jnp.float32),
        grid=(rows // TILE_ROWS,),
        in_specs=[
            spec_block,
            phase_block,
            phase_block,
            pl.BlockSpec((2, 2, TILE_ROWS, 1), lambda i: (0, 0, i, 0)),
            pl.BlockSpec((2, 2, 1, columns), lambda i: (0, 0, 0, 0)),
        ],
        out_specs=spec_block,
    )(spectrum, jnp.cos(phase_rows), jnp.sin(phase_rows), row_turn, column_turn)


def per_device(voltage, chirp_phase):
    groups = lax.axis_size("fft")
    device = lax.axis_index("fft")
    quarter = voltage.shape[2]
    row_count = 4 * quarter
    local_width = voltage.shape[3]
    columns = local_width * groups
    second_len = columns // B1
    total_bins = row_count * columns
    half_count = row_count // (2 * groups)
    local_rows = 2 * half_count
    is_first = device == 0
    row_order = fold_order(row_count, groups)
    local_order = lax.dynamic_slice_in_dim(row_order, device * local_rows, local_rows)
    first_range = jnp.arange(B1, dtype=jnp.int32)
    second_range = jnp.arange(second_len, dtype=jnp.int32)
    column_range = jnp.arange(columns, dtype=jnp.int32)
    sample_rows = jnp.arange(quarter, dtype=jnp.int32)
    entry_table = real_table(rotation(sample_rows[:, None] * row_order[None, :], row_count))
    samples_in = voltage[0].reshape(2, quarter, B1 // groups, second_len)
    entry_blocks = entry_table.reshape(2, 2, quarter, groups, local_rows)
    device_turn = rotation(row_order * (device * local_width), total_bins)
    block_range = jnp.arange(B1 // groups, dtype=jnp.int32)
    within_turn = rotation(row_order[:, None] * (second_len * block_range)[None, :], total_bins)
    inner_turn = rotation(row_order[:, None] * second_range[None, :], total_bins)
    outer_turn = complex_mul(device_turn[:, :, None], within_turn)
    turn = complex_mul(outer_turn[..., None], inner_turn[:, :, None, :])
    turn = turn.reshape(2, groups, local_rows, B1 // groups, second_len)
    spread = jnp.einsum("pmun,pqmdr->dqrun", samples_in, entry_blocks, precision=HIGH)
    spread = jnp.stack([
        spread[:, 0] * turn[0] - spread[:, 1] * turn[1],
        spread[:, 0] * turn[1] + spread[:, 1] * turn[0],
    ], axis=1)
    gathered = lax.all_to_all(spread, "fft", split_axis=0, concat_axis=0, tiled=True)
    gathered = gathered.reshape(groups, 2, 2, half_count, B1 // groups, second_len)
    section_one = both_halves(first_range, first_range, B1, False, True)
    block_turn = both_halves(first_range, second_range, columns, True, False)
    section_two = both_halves(second_range, second_range, second_len, False, True)
    first_blocks = real_table(section_one).reshape(2, 2, 2, groups, B1 // groups, B1)
    gathered = jnp.einsum("sphrun,pqhsuk->qhrkn", gathered, first_blocks, precision=HIGH)
    gathered = complex_mul(gathered, block_turn[:, :, None])
    spectrum = jnp.einsum("phrkn,pqhnj->qhrjk", gathered, real_table(section_two), precision=HIGH)
    spectrum = spectrum.reshape(2, 2, half_count, columns)
    half_rows = jnp.stack([local_order[:half_count], local_order[half_count:]])
    row_turn = rotation(half_rows, 2 * total_bins)[..., None]
    stored_columns = jnp.stack([column_range, columns - 1 - column_range])
    column_turn = rotation(stored_columns, 2 * columns)[:, :, None, :]
    phase_rows = jnp.stack([chirp_phase[0], reverse_lanes(chirp_phase[1])])
    packed = middle(spectrum, phase_rows, row_turn, column_turn)
    first_spec = spectrum[:, :, 0]
    first_turn = complex_mul(row_turn[:, :, 0], column_turn[:, :, 0])
    live = jnp.stack([column_range > 0, column_range >= 0])
    first_partner = jnp.stack(
        [jnp.roll(reverse_lanes(first_spec[:, 0]), 1, axis=-1), reverse_lanes(first_spec[:, 1])], axis=1
    )
    first_filtered = complex_mul(
        post_process(first_spec, conjugate(first_partner), first_turn),
        jnp.stack([jnp.cos(phase_rows[:, 0]), jnp.sin(phase_rows[:, 0])]),
    )
    first_filtered = jnp.where(live[None], first_filtered, 0.0)
    first_partner = jnp.stack(
        [jnp.roll(reverse_lanes(first_filtered[:, 0]), 1, axis=-1), reverse_lanes(first_filtered[:, 1])],
        axis=1,
    )
    first_packed = pre_process(first_filtered, conjugate(first_partner), first_turn)
    packed = packed.at[:, :, 0].set(jnp.where(is_first, first_packed, packed[:, :, 0]))
    packed = packed.reshape(2, 2, half_count, second_len, B1)
    back_two = both_halves(second_range, second_range, second_len, True, False)
    back_turn = both_halves(first_range, second_range, columns, True, False)
    back_one = both_halves(first_range, first_range, B1, True, False)
    packed = jnp.einsum(
        "phrjk,pqhjv->qhrkv", packed, real_table(conjugate(back_two)), precision=HIGH
    )
    packed = complex_mul(packed, conjugate(back_turn)[:, :, None])
    last_table = real_table(conjugate(back_one))
    packed = [
        jnp.einsum("phrkv,phku->hruv", packed, last_table[:, part], precision=HIGH).reshape(
            local_rows, B1, second_len
        )
        for part in (0, 1)
    ]
    upper_turn = rotation(local_order[:, None] * (second_len * first_range)[None, :], total_bins)
    lower_turn = rotation(local_order[:, None] * second_range[None, :], total_bins)
    back_row = complex_mul(upper_turn[..., None], lower_turn[:, :, None, :])
    signal_re = packed[0] * back_row[0] + packed[1] * back_row[1]
    signal_im = packed[1] * back_row[0] - packed[0] * back_row[1]
    signal_re = jnp.transpose(signal_re.reshape(local_rows, groups, local_width), (1, 0, 2))
    signal_im = jnp.transpose(signal_im.reshape(local_rows, groups, local_width), (1, 0, 2))
    packed = jnp.stack([signal_re, signal_im], axis=1)
    arrived = lax.all_to_all(packed, "fft", split_axis=0, concat_axis=0, tiled=True)
    arrived = jnp.transpose(arrived, (1, 0, 2, 3)).reshape(2, row_count, local_width)
    exit_turn = rotation(
        row_order[:, None] * jnp.arange(row_count, dtype=jnp.int32)[None, :], row_count
    )
    exit_table = real_table(jnp.stack([exit_turn[0] / total_bins, -exit_turn[1] / total_bins]))

    def sample_block(block_id):
        lower = block_id * quarter
        table = exit_table[:, :, :, lower : lower + quarter]
        return jnp.einsum("prn,pqrm->qmn", arrived, table, precision=HIGH)

    running = sample_block(3)
    for block_id in (2, 1, 0):
        running = sample_block(block_id) + passed_along(running, "seg", 1)
    return running[None]


def solution(mesh):
    in_specs = (P("seg", None, None, "fft"), P(None, "fft", None))
    out_specs = P("seg", None, None, "fft")
    return jax.shard_map(
        per_device, mesh=mesh, in_specs=in_specs, out_specs=out_specs, check_vma=False
    )
```

```python
import math

import jax
import jax.numpy as jnp
from jax import lax
from jax.experimental import pallas as pl
from jax.sharding import PartitionSpec as P

B1 = 64
TILE_ROWS = 8


HIGHEST = lax.Precision.HIGHEST
HIGH = lax.Precision.HIGH


def passed_along(shard, axis, by):
    length = lax.axis_size(axis)
    pairs = [(i, i + by) for i in range(length) if 0 <= i + by < length]
    return lax.ppermute(shard, axis, pairs)


def rotation(products, period):
    reduced = jnp.mod(products, period).astype(jnp.float32)
    angles = reduced * jnp.float32(-2.0 * math.pi / period)
    return jnp.stack([jnp.cos(angles), jnp.sin(angles)])


def conjugate(pair):
    return jnp.stack([pair[0], -pair[1]])


def real_table(pair):
    return jnp.stack([jnp.stack([pair[0], pair[1]]), jnp.stack([-pair[1], pair[0]])])


def complex_mul(left_pair, right_pair):
    first = left_pair[0] * right_pair[0] - left_pair[1] * right_pair[1]
    second = left_pair[0] * right_pair[1] + left_pair[1] * right_pair[0]
    return jnp.stack([first, second])


def fold_order(row_count, groups):
    half_count = row_count // (2 * groups)
    places = jnp.arange(row_count, dtype=jnp.int32)
    within = places % (2 * half_count)
    base_row = places // (2 * half_count) * half_count + within % half_count
    mirror_row = jnp.where(base_row > 0, row_count - base_row, row_count // 2)
    return jnp.where(within >= half_count, mirror_row, base_row)


def both_halves(outer, inner, period, reverse_outer, reverse_inner):
    last_outer = outer.shape[0] - 1
    last_inner = inner.shape[0] - 1
    natural = outer[:, None] * inner[None, :]
    outer_turned = (last_outer - outer) if reverse_outer else outer
    inner_turned = (last_inner - inner) if reverse_inner else inner
    turned = outer_turned[:, None] * inner_turned[None, :]
    return jnp.stack([rotation(natural, period), rotation(turned, period)], axis=1)


def reverse_lanes(values):
    width = values.shape[-1]
    tiles = values.reshape(values.shape[:-1] + (width // 128, 128))
    tiles = jnp.flip(tiles, axis=-2)
    lane = jnp.arange(128, dtype=jnp.int32)
    anti = (lane[:, None] + lane[None, :] == 127).astype(jnp.float32)
    flipped = jnp.einsum("...l,lm->...m", tiles, anti, precision=HIGHEST)
    return flipped.reshape(values.shape)


def partners(base, mirror, is_first):
    first_base = jnp.roll(reverse_lanes(base[:, 0]), 1, axis=-1)
    first_mirror = reverse_lanes(mirror[:, 0])
    of_base = mirror.at[:, 0].set(jnp.where(is_first, first_base, mirror[:, 0]))
    of_mirror = base.at[:, 0].set(jnp.where(is_first, first_mirror, base[:, 0]))
    return of_base, of_mirror


def post_process(spec, partner, turn):
    even = 0.5 * (spec + partner)
    odd = jnp.stack([0.5 * (spec[1] - partner[1]), -0.5 * (spec[0] - partner[0])])
    return even + complex_mul(odd, turn)


def pre_process(filtered, partner, turn):
    even_back = 0.5 * (filtered + partner)
    odd_back = complex_mul(0.5 * (filtered - partner), conjugate(turn))
    return jnp.stack([even_back[0] - odd_back[1], even_back[1] + odd_back[0]])


def middle_kernel(spec_ref, cos_ref, sin_ref, row_ref, column_ref, out_ref):
    turn_re = row_ref[0] * column_ref[0] - row_ref[1] * column_ref[1]
    turn_im = row_ref[0] * column_ref[1] + row_ref[1] * column_ref[0]
    filtered = []
    for half in (0, 1):
        other = 1 - half
        spec = jnp.stack([spec_ref[0, half], spec_ref[1, half]])
        partner = jnp.stack([spec_ref[0, other], -spec_ref[1, other]])
        turn = jnp.stack([turn_re[half], turn_im[half]])
        transformed = post_process(spec, partner, turn)
        filtered.append(complex_mul(transformed, jnp.stack([cos_ref[half], sin_ref[half]])))
    for half in (0, 1):
        other = filtered[1 - half]
        turn = jnp.stack([turn_re[half], turn_im[half]])
        packed = pre_process(filtered[half], conjugate(other), turn)
        out_ref[0, half] = packed[0]
        out_ref[1, half] = packed[1]


def middle(spectrum, phase_rows, row_turn, column_turn):
    shape = spectrum.shape
    tile = (TILE_ROWS,) + shape[3:]
    spec_block = pl.BlockSpec((2, 2) + tile, lambda i: (0, 0, i, 0, 0))
    phase_block = pl.BlockSpec((2,) + tile, lambda i: (0, i, 0, 0))
    phase_rows = phase_rows.reshape((2,) + shape[2:])
    return pl.pallas_call(
        middle_kernel,
        out_shape=jax.ShapeDtypeStruct(shape, jnp.float32),
        grid=(shape[2] // TILE_ROWS,),
        in_specs=[
            spec_block,
            phase_block,
            phase_block,
            pl.BlockSpec((2, 2, TILE_ROWS, 1, 1), lambda i: (0, 0, i, 0, 0)),
            pl.BlockSpec((2, 2, 1) + shape[3:], lambda i: (0, 0, 0, 0, 0)),
        ],
        out_specs=spec_block,
    )(
        spectrum,
        jnp.cos(phase_rows),
        jnp.sin(phase_rows),
        row_turn[..., None],
        column_turn.reshape((2, 2, 1) + shape[3:]),
    )


def per_device(voltage, chirp_phase):
    groups = lax.axis_size("fft")
    device = lax.axis_index("fft")
    quarter = voltage.shape[2]
    row_count = 4 * quarter
    local_width = voltage.shape[3]
    columns = local_width * groups
    second_len = columns // B1
    total_bins = row_count * columns
    half_count = row_count // (2 * groups)
    local_rows = 2 * half_count
    is_first = device == 0
    row_order = fold_order(row_count, groups)
    local_order = lax.dynamic_slice_in_dim(row_order, device * local_rows, local_rows)
    first_range = jnp.arange(B1, dtype=jnp.int32)
    second_range = jnp.arange(second_len, dtype=jnp.int32)
    column_range = jnp.arange(columns, dtype=jnp.int32)
    sample_rows = jnp.arange(quarter, dtype=jnp.int32)
    entry_table = real_table(rotation(sample_rows[:, None] * row_order[None, :], row_count))
    samples_in = voltage[0].reshape(2, quarter, B1 // groups, second_len)
    entry_blocks = entry_table.reshape(2, 2, quarter, groups, local_rows)
    device_turn = rotation(row_order * (device * local_width), total_bins)
    block_range = jnp.arange(B1 // groups, dtype=jnp.int32)
    within_turn = rotation(row_order[:, None] * (second_len * block_range)[None, :], total_bins)
    inner_turn = rotation(row_order[:, None] * second_range[None, :], total_bins)
    outer_turn = complex_mul(device_turn[:, :, None], within_turn)
    turn = complex_mul(outer_turn[..., None], inner_turn[:, :, None, :])
    turn = turn.reshape(2, groups, local_rows, B1 // groups, second_len)
    spread = jnp.einsum("pmun,pqmdr->dqrun", samples_in, entry_blocks, precision=HIGH)
    spread = jnp.stack([
        spread[:, 0] * turn[0] - spread[:, 1] * turn[1],
        spread[:, 0] * turn[1] + spread[:, 1] * turn[0],
    ], axis=1)
    gathered = lax.all_to_all(spread, "fft", split_axis=0, concat_axis=0, tiled=True)
    gathered = gathered.reshape(groups, 2, 2, half_count, B1 // groups, second_len)
    section_one = both_halves(first_range, first_range, B1, False, True)
    block_turn = both_halves(first_range, second_range, columns, True, False)
    section_two = both_halves(second_range, second_range, second_len, False, True)
    first_blocks = real_table(section_one).reshape(2, 2, 2, groups, B1 // groups, B1)
    gathered = jnp.einsum("sphrun,pqhsuk->qhrkn", gathered, first_blocks, precision=HIGH)
    gathered = complex_mul(gathered, block_turn[:, :, None])
    spectrum = jnp.einsum("phrkn,pqhnj->qhrjk", gathered, real_table(section_two), precision=HIGH)
    half_rows = jnp.stack([local_order[:half_count], local_order[half_count:]])
    row_turn = rotation(half_rows, 2 * total_bins)[..., None]
    stored_columns = jnp.stack([column_range, columns - 1 - column_range])
    column_turn = rotation(stored_columns, 2 * columns)[:, :, None, :]
    phase_rows = jnp.stack([chirp_phase[0], reverse_lanes(chirp_phase[1])])
    packed = middle(spectrum, phase_rows, row_turn, column_turn)
    first_spec = spectrum[:, :, 0].reshape(2, 2, columns)
    first_turn = complex_mul(row_turn[:, :, 0], column_turn[:, :, 0])
    live = jnp.stack([column_range > 0, column_range >= 0])
    first_partner = jnp.stack(
        [jnp.roll(reverse_lanes(first_spec[:, 0]), 1, axis=-1), reverse_lanes(first_spec[:, 1])], axis=1
    )
    first_filtered = complex_mul(
        post_process(first_spec, conjugate(first_partner), first_turn),
        jnp.stack([jnp.cos(phase_rows[:, 0]), jnp.sin(phase_rows[:, 0])]),
    )
    first_filtered = jnp.where(live[None], first_filtered, 0.0)
    first_partner = jnp.stack(
        [jnp.roll(reverse_lanes(first_filtered[:, 0]), 1, axis=-1), reverse_lanes(first_filtered[:, 1])],
        axis=1,
    )
    first_packed = pre_process(first_filtered, conjugate(first_partner), first_turn)
    first_packed = first_packed.reshape(2, 2, second_len, B1)
    packed = packed.at[:, :, 0].set(jnp.where(is_first, first_packed, packed[:, :, 0]))
    back_two = both_halves(second_range, second_range, second_len, True, False)
    back_turn = both_halves(first_range, second_range, columns, True, False)
    back_one = both_halves(first_range, first_range, B1, True, False)
    packed = jnp.einsum(
        "phrjk,pqhjv->qhrkv", packed, real_table(conjugate(back_two)), precision=HIGH
    )
    packed = complex_mul(packed, conjugate(back_turn)[:, :, None])
    last_table = real_table(conjugate(back_one))
    packed = [
        jnp.einsum("phrkv,phku->hruv", packed, last_table[:, part], precision=HIGH).reshape(
            local_rows, B1, second_len
        )
        for part in (0, 1)
    ]
    upper_turn = rotation(local_order[:, None] * (second_len * first_range)[None, :], total_bins)
    lower_turn = rotation(local_order[:, None] * second_range[None, :], total_bins)
    back_row = complex_mul(upper_turn[..., None], lower_turn[:, :, None, :])
    signal_re = packed[0] * back_row[0] + packed[1] * back_row[1]
    signal_im = packed[1] * back_row[0] - packed[0] * back_row[1]
    signal_re = jnp.transpose(signal_re.reshape(local_rows, groups, local_width), (1, 0, 2))
    signal_im = jnp.transpose(signal_im.reshape(local_rows, groups, local_width), (1, 0, 2))
    packed = jnp.stack([signal_re, signal_im], axis=1)
    arrived = lax.all_to_all(packed, "fft", split_axis=0, concat_axis=0, tiled=True)
    arrived = jnp.transpose(arrived, (1, 0, 2, 3)).reshape(2, row_count, local_width)
    exit_turn = rotation(
        row_order[:, None] * jnp.arange(row_count, dtype=jnp.int32)[None, :], row_count
    )
    exit_table = real_table(jnp.stack([exit_turn[0] / total_bins, -exit_turn[1] / total_bins]))

    def sample_block(block_id):
        lower = block_id * quarter
        table = exit_table[:, :, :, lower : lower + quarter]
        return jnp.einsum("prn,pqrm->qmn", arrived, table, precision=HIGH)

    running = sample_block(3)
    for block_id in (2, 1, 0):
        running = sample_block(block_id) + passed_along(running, "seg", 1)
    return running[None]


def solution(mesh):
    in_specs = (P("seg", None, None, "fft"), P(None, "fft", None))
    out_specs = P("seg", None, None, "fft")
    return jax.shard_map(
        per_device, mesh=mesh, in_specs=in_specs, out_specs=out_specs, check_vma=False
    )
```

```python
import math

import jax
import jax.numpy as jnp
from jax import lax
from jax.experimental import pallas as pl
from jax.sharding import PartitionSpec as P

B1 = 64
TILE_ROWS = 16


HIGHEST = lax.Precision.HIGHEST
HIGH = lax.Precision.HIGH


def passed_along(shard, axis, by):
    length = lax.axis_size(axis)
    pairs = [(i, i + by) for i in range(length) if 0 <= i + by < length]
    return lax.ppermute(shard, axis, pairs)


def rotation(products, period):
    reduced = jnp.mod(products, period).astype(jnp.float32)
    angles = reduced * jnp.float32(-2.0 * math.pi / period)
    return jnp.stack([jnp.cos(angles), jnp.sin(angles)])


def conjugate(pair):
    return jnp.stack([pair[0], -pair[1]])


def real_table(pair):
    return jnp.stack([jnp.stack([pair[0], pair[1]]), jnp.stack([-pair[1], pair[0]])])


def complex_mul(left_pair, right_pair):
    first = left_pair[0] * right_pair[0] - left_pair[1] * right_pair[1]
    second = left_pair[0] * right_pair[1] + left_pair[1] * right_pair[0]
    return jnp.stack([first, second])


def fold_order(row_count, groups):
    half_count = row_count // (2 * groups)
    places = jnp.arange(row_count, dtype=jnp.int32)
    within = places % (2 * half_count)
    base_row = places // (2 * half_count) * half_count + within % half_count
    mirror_row = jnp.where(base_row > 0, row_count - base_row, row_count // 2)
    return jnp.where(within >= half_count, mirror_row, base_row)


def both_halves(outer, inner, period, reverse_outer, reverse_inner):
    last_outer = outer.shape[0] - 1
    last_inner = inner.shape[0] - 1
    natural = outer[:, None] * inner[None, :]
    outer_turned = (last_outer - outer) if reverse_outer else outer
    inner_turned = (last_inner - inner) if reverse_inner else inner
    turned = outer_turned[:, None] * inner_turned[None, :]
    return jnp.stack([rotation(natural, period), rotation(turned, period)], axis=1)


def reverse_lanes(values):
    width = values.shape[-1]
    tiles = values.reshape(values.shape[:-1] + (width // 128, 128))
    tiles = jnp.flip(tiles, axis=-2)
    lane = jnp.arange(128, dtype=jnp.int32)
    anti = (lane[:, None] + lane[None, :] == 127).astype(jnp.float32)
    flipped = jnp.einsum("...l,lm->...m", tiles, anti, precision=HIGHEST)
    return flipped.reshape(values.shape)


def partners(base, mirror, is_first):
    first_base = jnp.roll(reverse_lanes(base[:, 0]), 1, axis=-1)
    first_mirror = reverse_lanes(mirror[:, 0])
    of_base = mirror.at[:, 0].set(jnp.where(is_first, first_base, mirror[:, 0]))
    of_mirror = base.at[:, 0].set(jnp.where(is_first, first_mirror, base[:, 0]))
    return of_base, of_mirror


def post_process(spec, partner, turn):
    even = 0.5 * (spec + partner)
    odd = jnp.stack([0.5 * (spec[1] - partner[1]), -0.5 * (spec[0] - partner[0])])
    return even + complex_mul(odd, turn)


def pre_process(filtered, partner, turn):
    even_back = 0.5 * (filtered + partner)
    odd_back = complex_mul(0.5 * (filtered - partner), conjugate(turn))
    return jnp.stack([even_back[0] - odd_back[1], even_back[1] + odd_back[0]])


def middle_kernel(spec_ref, cos_ref, sin_ref, row_ref, column_ref, out_ref):
    turn_re = row_ref[0] * column_ref[0] - row_ref[1] * column_ref[1]
    turn_im = row_ref[0] * column_ref[1] + row_ref[1] * column_ref[0]
    filtered = []
    for half in (0, 1):
        other = 1 - half
        spec = jnp.stack([spec_ref[0, half], spec_ref[1, half]])
        partner = jnp.stack([spec_ref[0, other], -spec_ref[1, other]])
        turn = jnp.stack([turn_re[half], turn_im[half]])
        transformed = post_process(spec, partner, turn)
        filtered.append(complex_mul(transformed, jnp.stack([cos_ref[half], sin_ref[half]])))
    for half in (0, 1):
        other = filtered[1 - half]
        turn = jnp.stack([turn_re[half], turn_im[half]])
        packed = pre_process(filtered[half], conjugate(other), turn)
        out_ref[0, half] = packed[0]
        out_ref[1, half] = packed[1]


def middle(spectrum, phase_rows, row_turn, column_turn):
    shape = spectrum.shape
    tile = (TILE_ROWS,) + shape[3:]
    spec_block = pl.BlockSpec((2, 2) + tile, lambda i: (0, 0, i, 0, 0))
    phase_block = pl.BlockSpec((2,) + tile, lambda i: (0, i, 0, 0))
    phase_rows = phase_rows.reshape((2,) + shape[2:])
    return pl.pallas_call(
        middle_kernel,
        out_shape=jax.ShapeDtypeStruct(shape, jnp.float32),
        grid=(shape[2] // TILE_ROWS,),
        in_specs=[
            spec_block,
            phase_block,
            phase_block,
            pl.BlockSpec((2, 2, TILE_ROWS, 1, 1), lambda i: (0, 0, i, 0, 0)),
            pl.BlockSpec((2, 2, 1) + shape[3:], lambda i: (0, 0, 0, 0, 0)),
        ],
        out_specs=spec_block,
    )(
        spectrum,
        jnp.cos(phase_rows),
        jnp.sin(phase_rows),
        row_turn[..., None],
        column_turn.reshape((2, 2, 1) + shape[3:]),
    )


def per_device(voltage, chirp_phase):
    groups = lax.axis_size("fft")
    device = lax.axis_index("fft")
    quarter = voltage.shape[2]
    row_count = 4 * quarter
    local_width = voltage.shape[3]
    columns = local_width * groups
    second_len = columns // B1
    total_bins = row_count * columns
    half_count = row_count // (2 * groups)
    local_rows = 2 * half_count
    is_first = device == 0
    row_order = fold_order(row_count, groups)
    local_order = lax.dynamic_slice_in_dim(row_order, device * local_rows, local_rows)
    first_range = jnp.arange(B1, dtype=jnp.int32)
    second_range = jnp.arange(second_len, dtype=jnp.int32)
    column_range = jnp.arange(columns, dtype=jnp.int32)
    sample_rows = jnp.arange(quarter, dtype=jnp.int32)
    entry_table = real_table(rotation(sample_rows[:, None] * row_order[None, :], row_count))
    samples_in = voltage[0].reshape(2, quarter, B1 // groups, second_len)
    entry_blocks = entry_table.reshape(2, 2, quarter, groups, local_rows)
    device_turn = rotation(row_order * (device * local_width), total_bins)
    block_range = jnp.arange(B1 // groups, dtype=jnp.int32)
    within_turn = rotation(row_order[:, None] * (second_len * block_range)[None, :], total_bins)
    inner_turn = rotation(row_order[:, None] * second_range[None, :], total_bins)
    outer_turn = complex_mul(device_turn[:, :, None], within_turn)
    turn = complex_mul(outer_turn[..., None], inner_turn[:, :, None, :])
    turn = turn.reshape(2, groups, local_rows, B1 // groups, second_len)
    spread = jnp.einsum("pmun,pqmdr->dqrun", samples_in, entry_blocks, precision=HIGH)
    spread = jnp.stack([
        spread[:, 0] * turn[0] - spread[:, 1] * turn[1],
        spread[:, 0] * turn[1] + spread[:, 1] * turn[0],
    ], axis=1)
    gathered = lax.all_to_all(spread, "fft", split_axis=0, concat_axis=0, tiled=True)
    gathered = gathered.reshape(groups, 2, 2, half_count, B1 // groups, second_len)
    section_one = both_halves(first_range, first_range, B1, False, True)
    block_turn = both_halves(first_range, second_range, columns, True, False)
    section_two = both_halves(second_range, second_range, second_len, False, True)
    first_blocks = real_table(section_one).reshape(2, 2, 2, groups, B1 // groups, B1)
    gathered = jnp.einsum("sphrun,pqhsuk->qhrkn", gathered, first_blocks, precision=HIGH)
    gathered = complex_mul(gathered, block_turn[:, :, None])
    spectrum = jnp.einsum("phrkn,pqhnj->qhrjk", gathered, real_table(section_two), precision=HIGH)
    half_rows = jnp.stack([local_order[:half_count], local_order[half_count:]])
    row_turn = rotation(half_rows, 2 * total_bins)[..., None]
    stored_columns = jnp.stack([column_range, columns - 1 - column_range])
    column_turn = rotation(stored_columns, 2 * columns)[:, :, None, :]
    phase_rows = jnp.stack([chirp_phase[0], reverse_lanes(chirp_phase[1])])
    packed = middle(spectrum, phase_rows, row_turn, column_turn)
    first_spec = spectrum[:, :, 0].reshape(2, 2, columns)
    first_turn = complex_mul(row_turn[:, :, 0], column_turn[:, :, 0])
    live = jnp.stack([column_range > 0, column_range >= 0])
    first_partner = jnp.stack(
        [jnp.roll(reverse_lanes(first_spec[:, 0]), 1, axis=-1), reverse_lanes(first_spec[:, 1])], axis=1
    )
    first_filtered = complex_mul(
        post_process(first_spec, conjugate(first_partner), first_turn),
        jnp.stack([jnp.cos(phase_rows[:, 0]), jnp.sin(phase_rows[:, 0])]),
    )
    first_filtered = jnp.where(live[None], first_filtered, 0.0)
    first_partner = jnp.stack(
        [jnp.roll(reverse_lanes(first_filtered[:, 0]), 1, axis=-1), reverse_lanes(first_filtered[:, 1])],
        axis=1,
    )
    first_packed = pre_process(first_filtered, conjugate(first_partner), first_turn)
    first_packed = first_packed.reshape(2, 2, second_len, B1)
    packed = packed.at[:, :, 0].set(jnp.where(is_first, first_packed, packed[:, :, 0]))
    back_two = both_halves(second_range, second_range, second_len, True, False)
    back_turn = both_halves(first_range, second_range, columns, True, False)
    back_one = both_halves(first_range, first_range, B1, True, False)
    packed = jnp.einsum(
        "phrjk,pqhjv->qhrkv", packed, real_table(conjugate(back_two)), precision=HIGH
    )
    packed = complex_mul(packed, conjugate(back_turn)[:, :, None])
    last_table = real_table(conjugate(back_one))
    packed = [
        jnp.einsum("phrkv,phku->hruv", packed, last_table[:, part], precision=HIGH).reshape(
            local_rows, B1, second_len
        )
        for part in (0, 1)
    ]
    upper_turn = rotation(local_order[:, None] * (second_len * first_range)[None, :], total_bins)
    lower_turn = rotation(local_order[:, None] * second_range[None, :], total_bins)
    back_row = complex_mul(upper_turn[..., None], lower_turn[:, :, None, :])
    signal_re = packed[0] * back_row[0] + packed[1] * back_row[1]
    signal_im = packed[1] * back_row[0] - packed[0] * back_row[1]
    signal_re = jnp.transpose(signal_re.reshape(local_rows, groups, local_width), (1, 0, 2))
    signal_im = jnp.transpose(signal_im.reshape(local_rows, groups, local_width), (1, 0, 2))
    packed = jnp.stack([signal_re, signal_im], axis=1)
    arrived = lax.all_to_all(packed, "fft", split_axis=0, concat_axis=0, tiled=True)
    arrived = jnp.transpose(arrived, (1, 0, 2, 3)).reshape(2, row_count, local_width)
    exit_turn = rotation(
        row_order[:, None] * jnp.arange(row_count, dtype=jnp.int32)[None, :], row_count
    )
    exit_table = real_table(jnp.stack([exit_turn[0] / total_bins, -exit_turn[1] / total_bins]))

    def sample_block(block_id):
        lower = block_id * quarter
        table = exit_table[:, :, :, lower : lower + quarter]
        return jnp.einsum("prn,pqrm->qmn", arrived, table, precision=HIGH)

    running = sample_block(3)
    for block_id in (2, 1, 0):
        running = sample_block(block_id) + passed_along(running, "seg", 1)
    return running[None]


def solution(mesh):
    in_specs = (P("seg", None, None, "fft"), P(None, "fft", None))
    out_specs = P("seg", None, None, "fft")
    return jax.shard_map(
        per_device, mesh=mesh, in_specs=in_specs, out_specs=out_specs, check_vma=False
    )
```

```python
import math

import jax
import jax.numpy as jnp
from jax import lax
from jax.experimental import pallas as pl
from jax.sharding import PartitionSpec as P

B1 = 64
TILE_ROWS = 8


HIGHEST = lax.Precision.HIGHEST
HIGH = lax.Precision.HIGH


def passed_along(shard, axis, by):
    length = lax.axis_size(axis)
    pairs = [(i, i + by) for i in range(length) if 0 <= i + by < length]
    return lax.ppermute(shard, axis, pairs)


def rotation(products, period):
    reduced = jnp.mod(products, period).astype(jnp.float32)
    angles = reduced * jnp.float32(-2.0 * math.pi / period)
    return jnp.stack([jnp.cos(angles), jnp.sin(angles)])


def conjugate(pair):
    return jnp.stack([pair[0], -pair[1]])


def real_table(pair):
    return jnp.stack([jnp.stack([pair[0], pair[1]]), jnp.stack([-pair[1], pair[0]])])


def complex_mul(left_pair, right_pair):
    first = left_pair[0] * right_pair[0] - left_pair[1] * right_pair[1]
    second = left_pair[0] * right_pair[1] + left_pair[1] * right_pair[0]
    return jnp.stack([first, second])


def fold_order(row_count, groups):
    half_count = row_count // (2 * groups)
    places = jnp.arange(row_count, dtype=jnp.int32)
    within = places % (2 * half_count)
    base_row = places // (2 * half_count) * half_count + within % half_count
    mirror_row = jnp.where(base_row > 0, row_count - base_row, row_count // 2)
    return jnp.where(within >= half_count, mirror_row, base_row)


def both_halves(outer, inner, period, reverse_outer, reverse_inner):
    last_outer = outer.shape[0] - 1
    last_inner = inner.shape[0] - 1
    natural = outer[:, None] * inner[None, :]
    outer_turned = (last_outer - outer) if reverse_outer else outer
    inner_turned = (last_inner - inner) if reverse_inner else inner
    turned = outer_turned[:, None] * inner_turned[None, :]
    return jnp.stack([rotation(natural, period), rotation(turned, period)], axis=1)


def reverse_lanes(values):
    width = values.shape[-1]
    tiles = values.reshape(values.shape[:-1] + (width // 128, 128))
    tiles = jnp.flip(tiles, axis=-2)
    lane = jnp.arange(128, dtype=jnp.int32)
    anti = (lane[:, None] + lane[None, :] == 127).astype(jnp.float32)
    flipped = jnp.einsum("...l,lm->...m", tiles, anti, precision=HIGHEST)
    return flipped.reshape(values.shape)


def partners(base, mirror, is_first):
    first_base = jnp.roll(reverse_lanes(base[:, 0]), 1, axis=-1)
    first_mirror = reverse_lanes(mirror[:, 0])
    of_base = mirror.at[:, 0].set(jnp.where(is_first, first_base, mirror[:, 0]))
    of_mirror = base.at[:, 0].set(jnp.where(is_first, first_mirror, base[:, 0]))
    return of_base, of_mirror


def post_process(spec, partner, turn):
    even = 0.5 * (spec + partner)
    odd = jnp.stack([0.5 * (spec[1] - partner[1]), -0.5 * (spec[0] - partner[0])])
    return even + complex_mul(odd, turn)


def pre_process(filtered, partner, turn):
    even_back = 0.5 * (filtered + partner)
    odd_back = complex_mul(0.5 * (filtered - partner), conjugate(turn))
    return jnp.stack([even_back[0] - odd_back[1], even_back[1] + odd_back[0]])


def middle_kernel(spec_ref, cos_ref, sin_ref, row_ref, column_ref, out_ref):
    turn_re = row_ref[0] * column_ref[0] - row_ref[1] * column_ref[1]
    turn_im = row_ref[0] * column_ref[1] + row_ref[1] * column_ref[0]
    filtered = []
    for half in (0, 1):
        other = 1 - half
        spec = jnp.stack([spec_ref[0, half], spec_ref[1, half]])
        partner = jnp.stack([spec_ref[0, other], -spec_ref[1, other]])
        turn = jnp.stack([turn_re[half], turn_im[half]])
        transformed = post_process(spec, partner, turn)
        filtered.append(complex_mul(transformed, jnp.stack([cos_ref[half], sin_ref[half]])))
    for half in (0, 1):
        other = filtered[1 - half]
        turn = jnp.stack([turn_re[half], turn_im[half]])
        packed = pre_process(filtered[half], conjugate(other), turn)
        out_ref[0, half] = packed[0]
        out_ref[1, half] = packed[1]


def middle(spectrum, phase_rows, row_turn, column_turn):
    shape = spectrum.shape
    tile = (TILE_ROWS,) + shape[3:]
    spec_block = pl.BlockSpec((2, 2) + tile, lambda i: (0, 0, i, 0, 0))
    phase_block = pl.BlockSpec((2,) + tile, lambda i: (0, i, 0, 0))
    phase_rows = phase_rows.reshape((2,) + shape[2:])
    return pl.pallas_call(
        middle_kernel,
        out_shape=jax.ShapeDtypeStruct(shape, jnp.float32),
        grid=(shape[2] // TILE_ROWS,),
        in_specs=[
            spec_block,
            phase_block,
            phase_block,
            pl.BlockSpec((2, 2, TILE_ROWS, 1, 1), lambda i: (0, 0, i, 0, 0)),
            pl.BlockSpec((2, 2, 1) + shape[3:], lambda i: (0, 0, 0, 0, 0)),
        ],
        out_specs=spec_block,
    )(
        spectrum,
        jnp.cos(phase_rows),
        jnp.sin(phase_rows),
        row_turn[..., None],
        column_turn.reshape((2, 2, 1) + shape[3:]),
    )


def per_device(voltage, chirp_phase):
    groups = lax.axis_size("fft")
    device = lax.axis_index("fft")
    quarter = voltage.shape[2]
    row_count = 4 * quarter
    local_width = voltage.shape[3]
    columns = local_width * groups
    second_len = columns // B1
    total_bins = row_count * columns
    half_count = row_count // (2 * groups)
    local_rows = 2 * half_count
    is_first = device == 0
    row_order = fold_order(row_count, groups)
    local_order = lax.dynamic_slice_in_dim(row_order, device * local_rows, local_rows)
    first_range = jnp.arange(B1, dtype=jnp.int32)
    second_range = jnp.arange(second_len, dtype=jnp.int32)
    column_range = jnp.arange(columns, dtype=jnp.int32)
    sample_rows = jnp.arange(quarter, dtype=jnp.int32)
    sixteen = jnp.arange(16, dtype=jnp.int32)
    entry_hi = rotation((16 * sixteen)[:, None] * row_order[None, :], row_count)
    entry_lo = rotation(sixteen[:, None] * row_order[None, :], row_count)
    entry_turn = complex_mul(entry_hi[:, :, None, :], entry_lo[:, None, :, :]).reshape(2, quarter, row_count)
    entry_table = real_table(entry_turn)
    samples_in = voltage[0].reshape(2, quarter, B1 // groups, second_len)
    entry_blocks = entry_table.reshape(2, 2, quarter, groups, local_rows)
    device_turn = rotation(row_order * (device * local_width), total_bins)
    block_range = jnp.arange(B1 // groups, dtype=jnp.int32)
    within_turn = rotation(row_order[:, None] * (second_len * block_range)[None, :], total_bins)
    inner_turn = rotation(row_order[:, None] * second_range[None, :], total_bins)
    outer_turn = complex_mul(device_turn[:, :, None], within_turn)
    turn = complex_mul(outer_turn[..., None], inner_turn[:, :, None, :])
    turn = turn.reshape(2, groups, local_rows, B1 // groups, second_len)
    spread = jnp.einsum("pmun,pqmdr->dqrun", samples_in, entry_blocks, precision=HIGH)
    spread = jnp.stack([
        spread[:, 0] * turn[0] - spread[:, 1] * turn[1],
        spread[:, 0] * turn[1] + spread[:, 1] * turn[0],
    ], axis=1)
    gathered = lax.all_to_all(spread, "fft", split_axis=0, concat_axis=0, tiled=True)
    gathered = gathered.reshape(groups, 2, 2, half_count, B1 // groups, second_len)
    section_one = both_halves(first_range, first_range, B1, False, True)
    block_turn = both_halves(first_range, second_range, columns, True, False)
    section_two = both_halves(second_range, second_range, second_len, False, True)
    first_blocks = real_table(section_one).reshape(2, 2, 2, groups, B1 // groups, B1)
    gathered = jnp.einsum("sphrun,pqhsuk->qhrkn", gathered, first_blocks, precision=HIGH)
    gathered = complex_mul(gathered, block_turn[:, :, None])
    spectrum = jnp.einsum("phrkn,pqhnj->qhrjk", gathered, real_table(section_two), precision=HIGH)
    half_rows = jnp.stack([local_order[:half_count], local_order[half_count:]])
    row_turn = rotation(half_rows, 2 * total_bins)[..., None]
    stored_columns = jnp.stack([column_range, columns - 1 - column_range])
    column_turn = rotation(stored_columns, 2 * columns)[:, :, None, :]
    phase_rows = jnp.stack([chirp_phase[0], reverse_lanes(chirp_phase[1])])
    packed = middle(spectrum, phase_rows, row_turn, column_turn)
    first_spec = spectrum[:, :, 0].reshape(2, 2, columns)
    first_turn = complex_mul(row_turn[:, :, 0], column_turn[:, :, 0])
    live = jnp.stack([column_range > 0, column_range >= 0])
    first_partner = jnp.stack(
        [jnp.roll(reverse_lanes(first_spec[:, 0]), 1, axis=-1), reverse_lanes(first_spec[:, 1])], axis=1
    )
    first_filtered = complex_mul(
        post_process(first_spec, conjugate(first_partner), first_turn),
        jnp.stack([jnp.cos(phase_rows[:, 0]), jnp.sin(phase_rows[:, 0])]),
    )
    first_filtered = jnp.where(live[None], first_filtered, 0.0)
    first_partner = jnp.stack(
        [jnp.roll(reverse_lanes(first_filtered[:, 0]), 1, axis=-1), reverse_lanes(first_filtered[:, 1])],
        axis=1,
    )
    first_packed = pre_process(first_filtered, conjugate(first_partner), first_turn)
    first_packed = first_packed.reshape(2, 2, second_len, B1)
    packed = packed.at[:, :, 0].set(jnp.where(is_first, first_packed, packed[:, :, 0]))
    back_two = both_halves(second_range, second_range, second_len, True, False)
    back_turn = both_halves(first_range, second_range, columns, True, False)
    back_one = both_halves(first_range, first_range, B1, True, False)
    packed = jnp.einsum(
        "phrjk,pqhjv->qhrkv", packed, real_table(conjugate(back_two)), precision=HIGH
    )
    packed = complex_mul(packed, conjugate(back_turn)[:, :, None])
    last_table = real_table(conjugate(back_one))
    packed = [
        jnp.einsum("phrkv,phku->hruv", packed, last_table[:, part], precision=HIGH).reshape(
            local_rows, B1, second_len
        )
        for part in (0, 1)
    ]
    upper_turn = rotation(local_order[:, None] * (second_len * first_range)[None, :], total_bins)
    lower_turn = rotation(local_order[:, None] * second_range[None, :], total_bins)
    back_row = complex_mul(upper_turn[..., None], lower_turn[:, :, None, :])
    signal_re = packed[0] * back_row[0] + packed[1] * back_row[1]
    signal_im = packed[1] * back_row[0] - packed[0] * back_row[1]
    signal_re = jnp.transpose(signal_re.reshape(local_rows, groups, local_width), (1, 0, 2))
    signal_im = jnp.transpose(signal_im.reshape(local_rows, groups, local_width), (1, 0, 2))
    packed = jnp.stack([signal_re, signal_im], axis=1)
    arrived = lax.all_to_all(packed, "fft", split_axis=0, concat_axis=0, tiled=True)
    arrived = jnp.transpose(arrived, (1, 0, 2, 3)).reshape(2, row_count, local_width)
    exit_turn = rotation(
        row_order[:, None] * jnp.arange(row_count, dtype=jnp.int32)[None, :], row_count
    )
    exit_table = real_table(jnp.stack([exit_turn[0] / total_bins, -exit_turn[1] / total_bins]))

    def sample_block(block_id):
        lower = block_id * quarter
        table = exit_table[:, :, :, lower : lower + quarter]
        return jnp.einsum("prn,pqrm->qmn", arrived, table, precision=HIGH)

    running = sample_block(3)
    for block_id in (2, 1, 0):
        running = sample_block(block_id) + passed_along(running, "seg", 1)
    return running[None]


def solution(mesh):
    in_specs = (P("seg", None, None, "fft"), P(None, "fft", None))
    out_specs = P("seg", None, None, "fft")
    return jax.shard_map(
        per_device, mesh=mesh, in_specs=in_specs, out_specs=out_specs, check_vma=False
    )
```

```python
import math

import jax
import jax.numpy as jnp
from jax import lax
from jax.experimental import pallas as pl
from jax.sharding import PartitionSpec as P

B1 = 64
TILE_ROWS = 8


HIGHEST = lax.Precision.HIGHEST
HIGH = lax.Precision.HIGH


def passed_along(shard, axis, by):
    length = lax.axis_size(axis)
    pairs = [(i, i + by) for i in range(length) if 0 <= i + by < length]
    return lax.ppermute(shard, axis, pairs)


def rotation(products, period):
    reduced = jnp.mod(products, period).astype(jnp.float32)
    angles = reduced * jnp.float32(-2.0 * math.pi / period)
    return jnp.stack([jnp.cos(angles), jnp.sin(angles)])


def conjugate(pair):
    return jnp.stack([pair[0], -pair[1]])


def real_table(pair):
    return jnp.stack([jnp.stack([pair[0], pair[1]]), jnp.stack([-pair[1], pair[0]])])


def complex_mul(left_pair, right_pair):
    first = left_pair[0] * right_pair[0] - left_pair[1] * right_pair[1]
    second = left_pair[0] * right_pair[1] + left_pair[1] * right_pair[0]
    return jnp.stack([first, second])


def fold_order(row_count, groups):
    half_count = row_count // (2 * groups)
    places = jnp.arange(row_count, dtype=jnp.int32)
    within = places % (2 * half_count)
    base_row = places // (2 * half_count) * half_count + within % half_count
    mirror_row = jnp.where(base_row > 0, row_count - base_row, row_count // 2)
    return jnp.where(within >= half_count, mirror_row, base_row)


def both_halves(outer, inner, period, reverse_outer, reverse_inner):
    last_outer = outer.shape[0] - 1
    last_inner = inner.shape[0] - 1
    natural = outer[:, None] * inner[None, :]
    outer_turned = (last_outer - outer) if reverse_outer else outer
    inner_turned = (last_inner - inner) if reverse_inner else inner
    turned = outer_turned[:, None] * inner_turned[None, :]
    return jnp.stack([rotation(natural, period), rotation(turned, period)], axis=1)


def reverse_lanes(values):
    width = values.shape[-1]
    tiles = values.reshape(values.shape[:-1] + (width // 128, 128))
    tiles = jnp.flip(tiles, axis=-2)
    lane = jnp.arange(128, dtype=jnp.int32)
    anti = (lane[:, None] + lane[None, :] == 127).astype(jnp.float32)
    flipped = jnp.einsum("...l,lm->...m", tiles, anti, precision=HIGHEST)
    return flipped.reshape(values.shape)


def partners(base, mirror, is_first):
    first_base = jnp.roll(reverse_lanes(base[:, 0]), 1, axis=-1)
    first_mirror = reverse_lanes(mirror[:, 0])
    of_base = mirror.at[:, 0].set(jnp.where(is_first, first_base, mirror[:, 0]))
    of_mirror = base.at[:, 0].set(jnp.where(is_first, first_mirror, base[:, 0]))
    return of_base, of_mirror


def post_process(spec, partner, turn):
    even = 0.5 * (spec + partner)
    odd = jnp.stack([0.5 * (spec[1] - partner[1]), -0.5 * (spec[0] - partner[0])])
    return even + complex_mul(odd, turn)


def pre_process(filtered, partner, turn):
    even_back = 0.5 * (filtered + partner)
    odd_back = complex_mul(0.5 * (filtered - partner), conjugate(turn))
    return jnp.stack([even_back[0] - odd_back[1], even_back[1] + odd_back[0]])


def middle_kernel(spec_ref, cos_ref, sin_ref, row_ref, column_ref, out_ref):
    turn_re = row_ref[0] * column_ref[0] - row_ref[1] * column_ref[1]
    turn_im = row_ref[0] * column_ref[1] + row_ref[1] * column_ref[0]
    filtered = []
    for half in (0, 1):
        other = 1 - half
        spec = jnp.stack([spec_ref[0, half], spec_ref[1, half]])
        partner = jnp.stack([spec_ref[0, other], -spec_ref[1, other]])
        turn = jnp.stack([turn_re[half], turn_im[half]])
        transformed = post_process(spec, partner, turn)
        filtered.append(complex_mul(transformed, jnp.stack([cos_ref[half], sin_ref[half]])))
    for half in (0, 1):
        other = filtered[1 - half]
        turn = jnp.stack([turn_re[half], turn_im[half]])
        packed = pre_process(filtered[half], conjugate(other), turn)
        out_ref[0, half] = packed[0]
        out_ref[1, half] = packed[1]


def middle(spectrum, phase_rows, row_turn, column_turn):
    shape = spectrum.shape
    tile = (TILE_ROWS,) + shape[3:]
    spec_block = pl.BlockSpec((2, 2) + tile, lambda i: (0, 0, i, 0, 0))
    phase_block = pl.BlockSpec((2,) + tile, lambda i: (0, i, 0, 0))
    phase_rows = phase_rows.reshape((2,) + shape[2:])
    return pl.pallas_call(
        middle_kernel,
        out_shape=jax.ShapeDtypeStruct(shape, jnp.float32),
        grid=(shape[2] // TILE_ROWS,),
        in_specs=[
            spec_block,
            phase_block,
            phase_block,
            pl.BlockSpec((2, 2, TILE_ROWS, 1, 1), lambda i: (0, 0, i, 0, 0)),
            pl.BlockSpec((2, 2, 1) + shape[3:], lambda i: (0, 0, 0, 0, 0)),
        ],
        out_specs=spec_block,
    )(
        spectrum,
        jnp.cos(phase_rows),
        jnp.sin(phase_rows),
        row_turn[..., None],
        column_turn.reshape((2, 2, 1) + shape[3:]),
    )


def per_device(voltage, chirp_phase):
    groups = lax.axis_size("fft")
    device = lax.axis_index("fft")
    quarter = voltage.shape[2]
    row_count = 4 * quarter
    local_width = voltage.shape[3]
    columns = local_width * groups
    second_len = columns // B1
    total_bins = row_count * columns
    half_count = row_count // (2 * groups)
    local_rows = 2 * half_count
    is_first = device == 0
    row_order = fold_order(row_count, groups)
    local_order = lax.dynamic_slice_in_dim(row_order, device * local_rows, local_rows)
    first_range = jnp.arange(B1, dtype=jnp.int32)
    second_range = jnp.arange(second_len, dtype=jnp.int32)
    column_range = jnp.arange(columns, dtype=jnp.int32)
    sample_rows = jnp.arange(quarter, dtype=jnp.int32)
    sixteen = jnp.arange(16, dtype=jnp.int32)
    entry_hi = rotation((16 * sixteen)[:, None] * row_order[None, :], row_count)
    entry_lo = rotation(sixteen[:, None] * row_order[None, :], row_count)
    entry_turn = complex_mul(entry_hi[:, :, None, :], entry_lo[:, None, :, :]).reshape(2, quarter, row_count)
    entry_table = real_table(entry_turn)
    samples_in = voltage[0].reshape(2, quarter, B1 // groups, second_len)
    entry_blocks = entry_table.reshape(2, 2, quarter, groups, local_rows)
    spread = jnp.einsum("pmun,pqmdr->dqrun", samples_in, entry_blocks, precision=HIGH)
    gathered = lax.all_to_all(spread, "fft", split_axis=0, concat_axis=0, tiled=True)
    source_range = jnp.arange(groups, dtype=jnp.int32)
    block_range = jnp.arange(B1 // groups, dtype=jnp.int32)
    source_turn = rotation((local_width * source_range)[:, None] * local_order[None, :], total_bins)
    within_turn = rotation(local_order[:, None] * (second_len * block_range)[None, :], total_bins)
    inner_turn = rotation(local_order[:, None] * second_range[None, :], total_bins)
    turn = complex_mul(
        complex_mul(source_turn[..., None, None], within_turn[:, None, :, :, None]),
        inner_turn[:, None, :, None, :],
    )
    gathered = jnp.stack([
        gathered[:, 0] * turn[0] - gathered[:, 1] * turn[1],
        gathered[:, 0] * turn[1] + gathered[:, 1] * turn[0],
    ], axis=1)
    gathered = gathered.reshape(groups, 2, 2, half_count, B1 // groups, second_len)
    section_one = both_halves(first_range, first_range, B1, False, True)
    block_turn = both_halves(first_range, second_range, columns, True, False)
    section_two = both_halves(second_range, second_range, second_len, False, True)
    first_blocks = real_table(section_one).reshape(2, 2, 2, groups, B1 // groups, B1)
    gathered = jnp.einsum("sphrun,pqhsuk->qhrkn", gathered, first_blocks, precision=HIGH)
    gathered = complex_mul(gathered, block_turn[:, :, None])
    spectrum = jnp.einsum("phrkn,pqhnj->qhrjk", gathered, real_table(section_two), precision=HIGH)
    half_rows = jnp.stack([local_order[:half_count], local_order[half_count:]])
    row_turn = rotation(half_rows, 2 * total_bins)[..., None]
    stored_columns = jnp.stack([column_range, columns - 1 - column_range])
    column_turn = rotation(stored_columns, 2 * columns)[:, :, None, :]
    phase_rows = jnp.stack([chirp_phase[0], reverse_lanes(chirp_phase[1])])
    packed = middle(spectrum, phase_rows, row_turn, column_turn)
    first_spec = spectrum[:, :, 0].reshape(2, 2, columns)
    first_turn = complex_mul(row_turn[:, :, 0], column_turn[:, :, 0])
    live = jnp.stack([column_range > 0, column_range >= 0])
    first_partner = jnp.stack(
        [jnp.roll(reverse_lanes(first_spec[:, 0]), 1, axis=-1), reverse_lanes(first_spec[:, 1])], axis=1
    )
    first_filtered = complex_mul(
        post_process(first_spec, conjugate(first_partner), first_turn),
        jnp.stack([jnp.cos(phase_rows[:, 0]), jnp.sin(phase_rows[:, 0])]),
    )
    first_filtered = jnp.where(live[None], first_filtered, 0.0)
    first_partner = jnp.stack(
        [jnp.roll(reverse_lanes(first_filtered[:, 0]), 1, axis=-1), reverse_lanes(first_filtered[:, 1])],
        axis=1,
    )
    first_packed = pre_process(first_filtered, conjugate(first_partner), first_turn)
    first_packed = first_packed.reshape(2, 2, second_len, B1)
    packed = packed.at[:, :, 0].set(jnp.where(is_first, first_packed, packed[:, :, 0]))
    back_two = both_halves(second_range, second_range, second_len, True, False)
    back_turn = both_halves(first_range, second_range, columns, True, False)
    back_one = both_halves(first_range, first_range, B1, True, False)
    packed = jnp.einsum(
        "phrjk,pqhjv->qhrkv", packed, real_table(conjugate(back_two)), precision=HIGH
    )
    packed = complex_mul(packed, conjugate(back_turn)[:, :, None])
    last_table = real_table(conjugate(back_one))
    packed = [
        jnp.einsum("phrkv,phku->hruv", packed, last_table[:, part], precision=HIGH).reshape(
            local_rows, B1, second_len
        )
        for part in (0, 1)
    ]
    upper_turn = rotation(local_order[:, None] * (second_len * first_range)[None, :], total_bins)
    lower_turn = rotation(local_order[:, None] * second_range[None, :], total_bins)
    back_row = complex_mul(upper_turn[..., None], lower_turn[:, :, None, :])
    signal_re = packed[0] * back_row[0] + packed[1] * back_row[1]
    signal_im = packed[1] * back_row[0] - packed[0] * back_row[1]
    signal_re = jnp.transpose(signal_re.reshape(local_rows, groups, local_width), (1, 0, 2))
    signal_im = jnp.transpose(signal_im.reshape(local_rows, groups, local_width), (1, 0, 2))
    packed = jnp.stack([signal_re, signal_im], axis=1)
    arrived = lax.all_to_all(packed, "fft", split_axis=0, concat_axis=0, tiled=True)
    arrived = jnp.transpose(arrived, (1, 0, 2, 3)).reshape(2, row_count, local_width)
    exit_turn = rotation(
        row_order[:, None] * jnp.arange(row_count, dtype=jnp.int32)[None, :], row_count
    )
    exit_table = real_table(jnp.stack([exit_turn[0] / total_bins, -exit_turn[1] / total_bins]))

    def sample_block(block_id):
        lower = block_id * quarter
        table = exit_table[:, :, :, lower : lower + quarter]
        return jnp.einsum("prn,pqrm->qmn", arrived, table, precision=HIGH)

    running = sample_block(3)
    for block_id in (2, 1, 0):
        running = sample_block(block_id) + passed_along(running, "seg", 1)
    return running[None]


def solution(mesh):
    in_specs = (P("seg", None, None, "fft"), P(None, "fft", None))
    out_specs = P("seg", None, None, "fft")
    return jax.shard_map(
        per_device, mesh=mesh, in_specs=in_specs, out_specs=out_specs, check_vma=False
    )
```
